512 devices in a mesh: half: 4 (over x_hi, core), wide: 128 (over z, y, x_lo).
Axes of the slice: x: 4 (x_hi: 2, x_lo: 2; x = x_hi * 2 + x_lo), y: 4, z: 16, core: 2. Of those that a mesh axis runs over, the one named last changes fastest.
Arguments:
- gains: float32 [4096, 4096], P(('half', 'wide')), parts along dimension 0, may hold values from -4 to 4
- response: bfloat16 [4096, 4096], P('wide', 'half'), parts along dimension 1, may hold values from -6 to 6
- student: bfloat16 [4096, 4096], P('wide', 'half'), parts along dimension 1, may hold values from 0.19921875 to 1
- blocks: bfloat16 [16, 256, 256], P('half'), parts along dimension 0, may hold values from -0.5 to 2.5, as said below
- order: int32 [4096], P('half'), parts along dimension 0, may hold values from 0 to 1023, each once
- lower: float32 [4096], P(('half', 'wide')), parts along dimension 0, may hold values from -1.2 to -0.4
- upper: float32 [4096], P(('half', 'wide')), parts along dimension 0, may hold values from 0.4 to 1.2
- lengths: float32 [4096], replicated, may hold values from 32 to 2048
- amplitude: float32 [4096], replicated, may hold values from 0.5 to 1.5
Outputs:
- tracked: float32 [4096, 4096], P(('half', 'wide')), parts along dimension 0
The draws below stay inside these ranges and needn't reach their ends.
There are 4 independent parts, one for each index of `half`. The reference program is written for one: setup_inputs(seed, part) draws one part's arguments, and reference() takes and returns one part's arrays. A program takes and returns all parts, laid end to end along the dimension named above; an argument that names none is the same for every part. Nothing has to cross between parts.
Inputs may be any that keep to these rules, and one draw needn't show every extreme that they name: `blocks`: each block is symmetric.
All inputs are finite; a program needn't handle non-finite values.
Results may differ from the reference program's by a relative error of at most 0.012.
The reference program's roundings to bfloat16 on the way (of `covar`, `packed` and `misfit`) count: a program that leaves them out, or rounds other values in their place, can miss the bound.
Values may be sent and summed in bfloat16 or wider, within the bound.
A program may use at most 128 MiB of HBM per device.

```python
import math
import jax
import jax.numpy as jnp

E = 4096
BLOCK = 256
NBLK = 4
ITERS = 2
CH = 1024


def draw_blocks(key, part):
    noise_key = jax.random.fold_in(key, 11)
    noise = jax.random.normal(noise_key, (NBLK, BLOCK, BLOCK), jnp.float32)
    scale = 1.0 / BLOCK ** 0.5
    diag = 1.5
    sym = (noise + jnp.swapaxes(noise, 1, 2)) * (scale / 2.0 ** 0.5)
    sym = jnp.clip(sym, -0.5, 0.5)
    eye = jnp.eye(BLOCK, dtype=jnp.float32)[None, :, :]
    return (sym + diag * eye).astype(jnp.bfloat16)


def steps_of(own_key, dims, shards, least, top_value):
    factor_of = 1.0
    for position, shards_of in shards:
        draws = jax.random.uniform(jax.random.fold_in(jax.random.fold_in(own_key, 6), position), (shards_of,), jnp.float32, least / len(shards), top_value / len(shards))
        factor_of = factor_of * jnp.repeat(jnp.exp(draws), dims[position] // shards_of).reshape((-1,) + (1,) * (len(dims) - 1 - position))
    return factor_of


def scatter_about(key, shape, spread, limit, cuts=(), kind=jnp.bfloat16):
    factor_of = steps_of(key, shape, cuts, -0.22, 0.18) if cuts else 1.0
    drawn = jax.random.normal(key, shape, jnp.float32) * spread * factor_of
    return jnp.minimum(jnp.maximum(drawn, -limit), limit).astype(kind)


def setup_inputs(seed: int = 0, part: int = 0) -> dict:
    streams_of = jax.random.split(jax.random.key(seed), 10)
    part_splits = jax.random.split(jax.random.fold_in(streams_of[9], part), 10)
    return {
        "gains": scatter_about(part_splits[0], (CH, E), 0.8, 4.0, ((0, 128),), jnp.float32),
        "response": scatter_about(part_splits[1], (E, CH), 1.0, 6.0, ((0, 128),)),
        "student": jnp.clip(jnp.exp(math.log(1.0) - 1.6133518 * jax.random.uniform(part_splits[2], (E, CH), jnp.float32) ** steps_of(part_splits[2], (E, CH), ((0, 128),), -0.2, 0.2)), 0.19921875, 1.0).astype(jnp.bfloat16),
        "blocks": draw_blocks(jax.random.fold_in(jax.random.fold_in(streams_of[9], part), 71), part),
        "order": jax.random.permutation(part_splits[4], CH).astype(jnp.int32),
        "lower": jnp.clip(-1.2 + 0.800000042 * jax.random.uniform(part_splits[5], (CH,), jnp.float32) ** steps_of(part_splits[5], (CH,), ((0, 128),), -0.2, 0.2), -1.2, -0.4),
        "upper": jnp.clip(0.4 + 0.800000042 * jax.random.uniform(part_splits[6], (CH,), jnp.float32) ** steps_of(part_splits[6], (CH,), ((0, 128),), -0.2, 0.2), 0.4, 1.2),
        "lengths": jnp.clip(jnp.exp(jax.random.uniform(streams_of[7], (E,), jnp.float32, math.log(32.0), math.log(2048.0))), 32.0, 2048.0),
        "amplitude": jnp.clip(jnp.exp(jax.random.uniform(streams_of[8], (E,), jnp.float32, math.log(0.5), math.log(1.5))), 0.5, 1.5),
    }


def build_covar(lengths, amplitude):
    count = lengths.shape[0]
    rows = jnp.arange(count, dtype=jnp.int32)
    diff = (rows[:, None] - rows[None, :]).astype(lengths.dtype)
    left = lengths[:, None]
    right = lengths[None, :]
    denom = left * left + right * right
    vals = amplitude[:, None] * amplitude[None, :] * jnp.sqrt(2.0 * left * right / denom) * jnp.exp(-diff * diff / denom)
    return vals.astype(jnp.bfloat16)

def reference(gains, response, student, blocks, order, lower, upper, lengths, amplitude):
    covar = build_covar(lengths, amplitude)
    chans = gains.shape[0]
    nblk = blocks.shape[0]
    width = blocks.shape[1]
    inverse = jnp.zeros((chans,), jnp.int32).at[order].set(jnp.arange(chans, dtype=jnp.int32))
    resp_perm = jnp.take(response, order, axis=1).astype(jnp.float32)
    stud_perm = jnp.take(student, order, axis=1).astype(jnp.float32)
    current = gains
    for step in range(ITERS):
        packed = current.astype(jnp.bfloat16).T
        moved = jnp.take(packed, order, axis=1).reshape(packed.shape[0], nblk, width)
        product = jnp.einsum('rbi,bij->rbj', moved.astype(jnp.float32), blocks.astype(jnp.float32)).reshape(packed.shape[0], chans)
        permuted = stud_perm * (product - resp_perm)
        misfit = jnp.take(permuted, inverse, axis=1).astype(jnp.bfloat16).T
        smoothed = jnp.dot(misfit, covar, preferred_element_type=jnp.float32)
        current = jnp.clip(current - 0.02 * smoothed, lower[:, None], upper[:, None])
    return current
```

```python
import functools

import jax
import jax.numpy as jnp
from jax import lax
from jax.experimental import pallas as pl
from jax.experimental.pallas import tpu as pltpu
from jax.sharding import PartitionSpec as P

ITERS = 2
F32 = jnp.float32
BF16 = jnp.bfloat16
NT = (((1,), (1,)), ((), ()))


def swap_blocks(parts, quarter):
    out = []
    for b in range(4):
        acc = None
        for g in range(4):
            moved = parts[g] if g == b else pltpu.roll(parts[g], (32 * (g - b)) % 128, 1)
            acc = moved if acc is None else jnp.where(quarter == g, moved, acc)
        out.append(acc)
    return out


def kernel(
    gains, bounds, response, student, blocks, order, lengths, amplitude, out,
    start_send, start_recv, state, bound_lo, bound_hi,
    pack_send, pack_recv, mis_send, mis_recv, gathered, final_send, final_recv,
    onehot, matrix, resp_tile, stud_tile, spread, covar, len_row, amp_row, len_col, amp_col, dist,
    plane_send_sem, plane_recv_sem, col_send_sem, col_recv_sem,
):
    wide = lax.axis_index("wide")
    z = wide // 8
    yx = wide % 8

    def at_plane(k):
        t = (yx + k) % 8
        return t, {"wide": z * 8 + t}

    def at_column(k):
        t = (z + k) % 16
        return t, {"wide": t * 8 + yx}

    barrier = pltpu.get_barrier_semaphore()
    for k in range(1, 16):
        _, dev = at_column(k)
        pl.semaphore_signal(barrier, inc=1, device_id=dev, device_id_type=pl.DeviceIdType.MESH)
    for k in range(1, 8):
        _, dev = at_plane(k)
        pl.semaphore_signal(barrier, inc=1, device_id=dev, device_id_type=pl.DeviceIdType.MESH)

    def remote(src, dst, ssem, rsem, dev):
        return pltpu.make_async_remote_copy(
            src_ref=src, dst_ref=dst, send_sem=ssem, recv_sem=rsem,
            device_id=dev, device_id_type=pl.DeviceIdType.MESH,
        )

    quarter8 = lax.broadcasted_iota(jnp.int32, (8, 128), 1) // 32
    quarter16 = lax.broadcasted_iota(jnp.int32, (16, 128), 1) // 32
    quarter256 = lax.broadcasted_iota(jnp.int32, (256, 128), 1) // 32

    for h in range(2):
        for a in range(4):
            parts = [gains[:, pl.ds(128 * (2 * (4 * a + b) + h), 128)] for b in range(4)]
            for c, y in enumerate(swap_blocks(parts, quarter8)):
                start_send[4 * h + c, :, pl.ds(128 * a, 128)] = y
    for t in range(8):
        start_send[t, :, pl.ds(512, 128)] = bounds[...]

    pl.semaphore_wait(barrier, 22)

    starts = []
    for k in range(1, 8):
        t, dev = at_plane(k)
        c = remote(start_send.at[t], start_recv.at[yx], plane_send_sem.at[0, k], plane_recv_sem.at[0, k], dev)
        c.start()
        starts.append(c)
    start_recv[yx] = start_send[yx]

    row = lax.broadcasted_iota(jnp.int32, (1024, 128), 0)
    chan = ((row // 16) % 16) * 64 + (row // 256) * 16 + row % 16
    for j in range(8):
        onehot[:, pl.ds(128 * j, 128)] = jnp.where(chan == order[pl.ds(j, 1), :], 1.0, 0.0).astype(BF16)

    @pl.loop(0, 4)
    def _(q):
        rows = pl.ds(pl.multiple_of(q * 256, 256), 256)
        for b in range(4):
            spread[:, pl.ds(256 * b, 256)] = jnp.dot(
                onehot[rows, pl.ds(256 * b, 256)], blocks[b], preferred_element_type=F32
            ).astype(BF16)
        matrix[rows, :] = lax.dot_general(
            spread[...], onehot[...], NT, preferred_element_type=F32
        ).astype(BF16)

    for c in starts:
        c.wait()
    for s in range(8):
        state[pl.ds(8 * s, 8), :] = start_recv[s, :, pl.ds(0, 512)]
        bound_lo[pl.ds(8 * s, 8), :] = jnp.broadcast_to(start_recv[s, :, pl.ds(512, 1)], (8, 128))
        bound_hi[pl.ds(8 * s, 8), :] = jnp.broadcast_to(start_recv[s, :, pl.ds(576, 1)], (8, 128))

    def send_column(it, which, send, recv):
        copies = []
        for k in (8, 7, 9, 6, 10, 5, 11, 4, 12, 3, 13, 2, 14, 1, 15):
            t, dev = at_column(k)
            c = remote(send.at[t], recv.at[it, z], col_send_sem.at[it, which, k], col_recv_sem.at[it, which, k], dev)
            c.start()
            copies.append(c)
        recv[it, z] = send[z]
        return copies

    def prepare_rest():
        for src, dst in ((response, resp_tile), (student, stud_tile)):
            x = src[...].astype(F32)
            tall = jnp.transpose(jnp.concatenate([x, x, x, x], axis=0))
            for t in range(16):
                acc = tall[64 * t : 64 * t + 16]
                for g in range(1, 4):
                    acc = jnp.where(quarter16 == g, tall[64 * t + 16 * g : 64 * t + 16 * g + 16], acc)
                dst[pl.ds(16 * t, 16), :] = acc

    def prepare_covar():
        quarter4 = lax.broadcasted_iota(jnp.int32, (4, 128), 1) // 32
        for src, dst in ((lengths, len_row), (amplitude, amp_row)):
            for h in range(2):
                parts = [
                    jnp.concatenate([src[pl.ds(h + 2 * b + 8 * a, 1), :] for a in range(4)], axis=0)
                    for b in range(4)
                ]
                for c, y in enumerate(swap_blocks(parts, quarter4)):
                    dst[4 * h + c, pl.ds(0, 4), :] = y
        own_len = len_row[yx]
        own_amp = amp_row[yx]
        for a in range(4):
            lc = jnp.transpose(jnp.broadcast_to(own_len[a : a + 1, :], (128, 128)))
            ac = jnp.transpose(jnp.broadcast_to(own_amp[a : a + 1, :], (128, 128)))
            len_col[a] = lc * lc
            amp_col[a] = ac * jnp.sqrt(2.0 * lc)
        i0 = lax.broadcasted_iota(jnp.int32, (128, 128), 0)
        i1 = lax.broadcasted_iota(jnp.int32, (128, 128), 1)
        dist[...] = ((i0 // 32 - i1 // 32) * 256 + i0 % 32 - i1 % 32).astype(F32)

        @pl.loop(0, 8)
        def _(t):
            lrow = len_row[t]
            arow = amp_row[t]
            for b in range(4):
                lr = lrow[b : b + 1, :]
                sq = lr * lr
                ar = arow[b : b + 1, :] * jnp.sqrt(lr)
                for a in range(4):
                    shift = ((a - b) * 1024 + (yx - t) * 32).astype(F32)
                    d = dist[...] + shift
                    inv = lax.rsqrt(len_col[a] + sq)
                    q = d * inv
                    vals = (amp_col[a] * ar) * (inv * jnp.exp(-(q * q)))
                    covar[pl.ds(128 * a, 128), pl.ds(pl.multiple_of(512 * t + 128 * b, 128), 128)] = vals.astype(BF16)

    for it in range(ITERS):
        for a in range(4):
            parts = [state[pl.ds(16 * g, 16), pl.ds(128 * a, 128)] for g in range(4)]
            for b, y in enumerate(swap_blocks(parts, quarter16)):
                pack_send[4 * a + b] = y.astype(BF16)
        copies = send_column(it, 0, pack_send, pack_recv)
        if it == 0:
            prepare_rest()
        for c in copies:
            c.wait()
        got = pack_recv[it].astype(F32).reshape(256, 128)
        for g in range(4):
            x = jnp.where(quarter256 == g, got, 0.0)
            x = x + pltpu.roll(x, 32, 1)
            x = x + pltpu.roll(x, 64, 1)
            spread[:, pl.ds(128 * g, 128)] = x.astype(BF16)
        prod = None
        for g2 in range(4):
            acc = None
            for g in range(4):
                p = jnp.dot(
                    matrix[pl.ds(256 * g2, 256), pl.ds(256 * g, 256)], spread[:, pl.ds(128 * g, 128)],
                    preferred_element_type=F32,
                )
                acc = p if acc is None else acc + p
            prod = acc if prod is None else jnp.where(quarter256 == g2, acc, prod)
        misfit = (stud_tile[...] * (prod - resp_tile[...])).astype(BF16)
        mis_send[...] = misfit.reshape(16, 16, 128)
        copies = send_column(it, 1, mis_send, mis_recv)
        if it == 0:
            prepare_covar()
        for c in copies:
            c.wait()
        for a in range(4):
            parts = [mis_recv[it, 4 * a + b].astype(F32) for b in range(4)]
            for g, y in enumerate(swap_blocks(parts, quarter16)):
                gathered[it, yx, pl.ds(16 * g, 16), pl.ds(128 * a, 128)] = y.astype(BF16)
        copies = []
        for k in range(1, 8):
            t, dev = at_plane(k)
            c = remote(
                gathered.at[it, yx], gathered.at[it, yx],
                plane_send_sem.at[1 + it, k], plane_recv_sem.at[1 + it, k], dev,
            )
            c.start()
            copies.append(c)
        smoothed = None
        for k in range(8):
            if k:
                copies[k - 1].wait_recv()
            t = (yx - k + 8) % 8
            p = lax.dot_general(
                gathered[it, t], covar[:, pl.ds(pl.multiple_of(512 * t, 512), 512)], NT,
                preferred_element_type=F32,
            )
            smoothed = p if smoothed is None else smoothed + p
        lo = jnp.concatenate([bound_lo[...]] * 4, axis=1)
        hi = jnp.concatenate([bound_hi[...]] * 4, axis=1)
        state[...] = jnp.minimum(jnp.maximum(state[...] - 0.02 * smoothed, lo), hi)
        for c in copies:
            c.wait_send()

    for s in range(8):
        final_send[s] = state[pl.ds(8 * s, 8), :]
    copies = []
    for k in range(1, 8):
        t, dev = at_plane(k)
        c = remote(final_send.at[t], final_recv.at[yx], plane_send_sem.at[3, k], plane_recv_sem.at[3, k], dev)
        c.start()
        copies.append(c)
    final_recv[yx] = final_send[yx]
    for c in copies:
        c.wait()
    for h in range(2):
        for a in range(4):
            parts = [final_recv[4 * h + c, :, pl.ds(128 * a, 128)] for c in range(4)]
            for b, y in enumerate(swap_blocks(parts, quarter8)):
                out[:, pl.ds(128 * (2 * (4 * a + b) + h), 128)] = y


def per_device(gains, response, student, blocks, order, lower, upper, lengths, amplitude):
    bounds = jnp.concatenate(
        [jnp.broadcast_to(lower[:, None], (8, 64)), jnp.broadcast_to(upper[:, None], (8, 64))], axis=1
    )
    vmem = pl.BlockSpec(memory_space=pltpu.VMEM)
    return pl.pallas_call(
        kernel,
        out_shape=jax.ShapeDtypeStruct((8, 4096), F32),
        in_specs=[vmem] * 8,
        out_specs=vmem,
        scratch_shapes=[
            pltpu.VMEM((8, 8, 640), F32),
            pltpu.VMEM((8, 8, 640), F32),
            pltpu.VMEM((64, 512), F32),
            pltpu.VMEM((64, 128), F32),
            pltpu.VMEM((64, 128), F32),
            pltpu.VMEM((16, 16, 128), BF16),
            pltpu.VMEM((ITERS, 16, 16, 128), BF16),
            pltpu.VMEM((16, 16, 128), BF16),
            pltpu.VMEM((ITERS, 16, 16, 128), BF16),
            pltpu.VMEM((ITERS, 8, 64, 512), BF16),
            pltpu.VMEM((8, 8, 512), F32),
            pltpu.VMEM((8, 8, 512), F32),
            pltpu.VMEM((1024, 1024), BF16),
            pltpu.VMEM((1024, 1024), BF16),
            pltpu.VMEM((256, 128), F32),
            pltpu.VMEM((256, 128), F32),
            pltpu.VMEM((256, 1024), BF16),
            pltpu.VMEM((512, 4096), BF16),
            pltpu.VMEM((8, 8, 128), F32),
            pltpu.VMEM((8, 8, 128), F32),
            pltpu.VMEM((4, 128, 128), F32),
            pltpu.VMEM((4, 128, 128), F32),
            pltpu.VMEM((128, 128), F32),
            pltpu.SemaphoreType.DMA((4, 8)),
            pltpu.SemaphoreType.DMA((4, 8)),
            pltpu.SemaphoreType.DMA((ITERS, 2, 16)),
            pltpu.SemaphoreType.DMA((ITERS, 2, 16)),
        ],
        compiler_params=pltpu.CompilerParams(collective_id=0, has_side_effects=True, vmem_limit_bytes=48 << 20),
        name="track",
    )(
        gains, bounds, response, student, blocks,
        order.reshape(8, 128), lengths.reshape(32, 128), amplitude.reshape(32, 128),
    )


def solution(mesh):
    placed = (
        P(("half", "wide"), None),
        P("wide", "half"),
        P("wide", "half"),
        P("half", None, None),
        P("half"),
        P(("half", "wide")),
        P(("half", "wide")),
        P(),
        P(),
    )
    return jax.shard_map(
        per_device, mesh=mesh, in_specs=placed, out_specs=P(("half", "wide"), None), check_vma=False
    )
```

```python
import functools

import jax
import jax.numpy as jnp
from jax import lax
from jax.experimental import pallas as pl
from jax.experimental.pallas import tpu as pltpu
from jax.sharding import PartitionSpec as P

ITERS = 2
F32 = jnp.float32
BF16 = jnp.bfloat16
STEP = 4
NEAR = tuple(range(-STEP, 0)) + tuple(range(1, STEP + 1))
NT = (((1,), (1,)), ((), ()))


def swap_blocks(parts, quarter):
    out = []
    for b in range(4):
        acc = None
        for g in range(4):
            moved = parts[g] if g == b else pltpu.roll(parts[g], (32 * (g - b)) % 128, 1)
            acc = moved if acc is None else jnp.where(quarter == g, moved, acc)
        out.append(acc)
    return out


def kernel(
    gains_hbm, lower_hbm, upper_hbm, response_hbm, student_hbm, blocks_hbm, order_hbm, lengths_hbm, amplitude_hbm,
    out,
    gains, lower, upper, response, student, blocks, order, lengths, amplitude,
    start_send, start_recv, bound_send, bound_recv, state,
    pack_send, pack_recv, mis_send, mis_recv, gathered, final_send, final_recv,
    onehot, matrix, resp_tile, stud_tile, spread, covar, len_abs, amp_abs, len_rel, amp_rel, len_col, amp_col, pos_col,
    load_sem, entry_sem, plane_send_sem, plane_recv_sem, ag_send_sem, ag_recv_sem, col_send_sem, col_recv_sem,
):
    wide = lax.axis_index("wide")
    z = wide // 8
    yx = wide % 8

    def at_plane(k):
        t = (yx + k) % 8
        return t, {"wide": z * 8 + t}

    def at_column(k):
        t = (z + k + 16) % 16
        return t, {"wide": t * 8 + yx}

    def signal(sem, dev):
        pl.semaphore_signal(sem, inc=1, device_id=dev, device_id_type=pl.DeviceIdType.MESH)

    barrier = pltpu.get_barrier_semaphore()
    for k in NEAR:
        signal(barrier, at_column(k)[1])
    for k in range(1, 8):
        signal(barrier, at_plane(k)[1])

    loads = []
    for n, (src, dst) in enumerate((
        (gains_hbm, gains), (order_hbm, order), (blocks_hbm, blocks), (lower_hbm, lower), (upper_hbm, upper),
        (lengths_hbm, lengths), (amplitude_hbm, amplitude), (response_hbm, response), (student_hbm, student),
    )):
        c = pltpu.make_async_copy(src, dst, load_sem.at[n])
        c.start()
        loads.append(c)

    def remote(src, dst, ssem, rsem, dev):
        return pltpu.make_async_remote_copy(
            src_ref=src, dst_ref=dst, send_sem=ssem, recv_sem=rsem,
            device_id=dev, device_id_type=pl.DeviceIdType.MESH,
        )

    quarter8 = lax.broadcasted_iota(jnp.int32, (8, 128), 1) // 32
    quarter16 = lax.broadcasted_iota(jnp.int32, (16, 128), 1) // 32
    quarter256 = lax.broadcasted_iota(jnp.int32, (256, 128), 1) // 32

    loads[0].wait()
    for h in range(2):
        for a in range(4):
            parts = [gains[:, pl.ds(128 * (2 * (4 * a + b) + h), 128)] for b in range(4)]
            for c, y in enumerate(swap_blocks(parts, quarter8)):
                start_send[4 * h + c, :, pl.ds(128 * a, 128)] = y

    pl.semaphore_wait(barrier, 7 + len(NEAR))
    for k in (STEP, -STEP):
        signal(entry_sem, at_column(k)[1])

    starts = []
    for k in range(1, 8):
        t, dev = at_plane(k)
        c = remote(start_send.at[t], start_recv.at[yx], plane_send_sem.at[0, k], plane_recv_sem.at[0, k], dev)
        c.start()
        starts.append(c)
    start_recv[yx] = start_send[yx]

    loads[1].wait()
    row = lax.broadcasted_iota(jnp.int32, (1024, 128), 0)
    chan = ((row // 16) % 16) * 64 + (row // 256) * 16 + row % 16
    for j in range(8):
        onehot[:, pl.ds(128 * j, 128)] = jnp.where(chan == order[pl.ds(j, 1), :], 1.0, 0.0).astype(BF16)
    loads[2].wait()

    @pl.loop(0, 4)
    def _(q):
        rows = pl.ds(pl.multiple_of(q * 256, 256), 256)
        for b in range(4):
            spread[:, pl.ds(256 * b, 256)] = jnp.dot(
                onehot[rows, pl.ds(256 * b, 256)], blocks[b], preferred_element_type=F32
            ).astype(BF16)
        matrix[rows, :] = lax.dot_general(
            spread[...], onehot[...], NT, preferred_element_type=F32
        ).astype(BF16)

    for c in starts:
        c.wait()
    pl.semaphore_wait(entry_sem, 2)

    def send_column(it, which, send, recv, slot):
        copies = {}
        for k in (8, 7, 9, 6, 10, 5, 11, 4, 12, 3, 13, 2, 14, 1, 15):
            t, dev = at_column(k)
            c = remote(
                send.at[t], recv.at[it, slot(k)], col_send_sem.at[it, which, k], col_recv_sem.at[it, which, k], dev
            )
            c.start()
            copies[k] = c
        recv[it, slot(0)] = send[z]
        return copies

    def send_bounds():
        loads[3].wait()
        loads[4].wait()
        i0 = lax.broadcasted_iota(jnp.int32, (8, 128), 0)
        left = lax.broadcasted_iota(jnp.int32, (8, 128), 1) < 64
        tile = jnp.zeros((8, 128), F32)
        for r in range(8):
            tile = jnp.where(i0 == r, jnp.where(left, lower[r], upper[r]), tile)
        bound_send[...] = tile
        copies = []
        for k in range(1, 8):
            _, dev = at_plane(k)
            c = remote(bound_send, bound_recv.at[yx], plane_send_sem.at[1, k], plane_recv_sem.at[1, k], dev)
            c.start()
            copies.append(c)
        bound_recv[yx] = tile
        return copies

    def prepare_rest():
        loads[7].wait()
        loads[8].wait()
        for src, dst in ((response, resp_tile), (student, stud_tile)):
            x = src[...].astype(F32)
            tall = jnp.transpose(jnp.concatenate([x, x, x, x], axis=0))
            for t in range(16):
                acc = tall[64 * t : 64 * t + 16]
                for g in range(1, 4):
                    acc = jnp.where(quarter16 == g, tall[64 * t + 16 * g : 64 * t + 16 * g + 16], acc)
                dst[pl.ds(16 * t, 16), :] = acc

    def prepare_rows():
        loads[5].wait()
        loads[6].wait()
        quarter1 = lax.broadcasted_iota(jnp.int32, (1, 128), 1) // 32
        for src, dst in ((lengths, len_abs), (amplitude, amp_abs)):
            for h in range(2):
                for a in range(4):
                    parts = [src[pl.ds(h + 2 * b + 8 * a, 1), :] for b in range(4)]
                    for c, y in enumerate(swap_blocks(parts, quarter1)):
                        dst[pl.ds(4 * h + c, 1), pl.ds(128 * a, 128)] = y
        turn = ((4 - z + 16) % 16) * 32
        len_all = len_abs[...]
        amp_all = amp_abs[...] * jnp.sqrt(len_all)
        len_rel[...] = pltpu.roll(len_all * len_all, turn, 1)
        amp_rel[...] = pltpu.roll(amp_all, turn, 1)
        own_len = len_abs[pl.ds(yx, 1), :]
        own_amp = amp_abs[pl.ds(yx, 1), :]
        i0 = lax.broadcasted_iota(jnp.int32, (128, 128), 0)
        for a in range(4):
            lc = jnp.transpose(jnp.broadcast_to(own_len[:, 128 * a : 128 * a + 128], (128, 128)))
            ac = jnp.transpose(jnp.broadcast_to(own_amp[:, 128 * a : 128 * a + 128], (128, 128)))
            len_col[a] = lc * lc
            amp_col[a] = ac * jnp.sqrt(2.0 * lc)
            pos_col[a] = ((4 * a + i0 // 32) * 256 + i0 % 32 + yx * 32).astype(F32)

    def prepare_covar(first, last):
        i1 = lax.broadcasted_iota(jnp.int32, (1, 512), 1)
        pos = (((i1 // 32 + z + 12) % 16) * 256 + i1 % 32).astype(F32)

        @pl.loop(first, last)
        def _(t):
            lrow = len_rel[pl.ds(t, 1), :]
            arow = amp_rel[pl.ds(t, 1), :]
            prow = pos + (t * 32).astype(F32)
            for b in range(4):
                lr = lrow[:, 128 * b : 128 * b + 128]
                ar = arow[:, 128 * b : 128 * b + 128]
                pr = prow[:, 128 * b : 128 * b + 128]
                for a in range(4):
                    inv = lax.rsqrt(len_col[a] + lr)
                    q = (pos_col[a] - pr) * inv
                    vals = (amp_col[a] * ar) * (inv * jnp.exp(-(q * q)))
                    covar[pl.ds(128 * a, 128), pl.ds(pl.multiple_of(512 * t + 128 * b, 128), 128)] = vals.astype(BF16)

    def slot_of_plane(k):
        return z

    def slot_of_piece(k):
        return (4 - k) % 16

    for it in range(ITERS):
        now = start_recv[...].reshape(64, 512) if it == 0 else state[...]
        for a in range(4):
            parts = [now[16 * g : 16 * g + 16, 128 * a : 128 * a + 128] for g in range(4)]
            for b, y in enumerate(swap_blocks(parts, quarter16)):
                pack_send[4 * a + b] = y.astype(BF16)
        copies = send_column(it, 0, pack_send, pack_recv, slot_of_plane)
        if it == 0:
            bounds = send_bounds()
            prepare_rest()
            prepare_rows()
            prepare_covar(0, 3)
        for c in copies.values():
            c.wait()
        got = pack_recv[it].astype(F32).reshape(256, 128)
        for g in range(4):
            x = jnp.where(quarter256 == g, got, 0.0)
            x = x + pltpu.roll(x, 32, 1)
            x = x + pltpu.roll(x, 64, 1)
            spread[:, pl.ds(128 * g, 128)] = x.astype(BF16)
        prod = None
        for g2 in range(4):
            acc = None
            for g in range(4):
                p = jnp.dot(
                    matrix[pl.ds(256 * g2, 256), pl.ds(256 * g, 256)], spread[:, pl.ds(128 * g, 128)],
                    preferred_element_type=F32,
                )
                acc = p if acc is None else acc + p
            prod = acc if prod is None else jnp.where(quarter256 == g2, acc, prod)
        misfit = (stud_tile[...] * (prod - resp_tile[...])).astype(BF16)
        mis_send[...] = misfit.reshape(16, 16, 128)
        copies = send_column(it, 1, mis_send, mis_recv, slot_of_piece)
        if it == 0:
            prepare_covar(3, 6)

        forwards = []
        for part in range(2):
            for k, c in copies.items():
                if slot_of_piece(k) // 8 == part:
                    c.wait_recv()
            for a in range(2):
                parts = [mis_recv[it, 8 * part + 4 * a + b].astype(F32) for b in range(4)]
                for g, y in enumerate(swap_blocks(parts, quarter16)):
                    gathered[it, yx, part, pl.ds(16 * g, 16), pl.ds(128 * a, 128)] = y.astype(BF16)
            sent = []
            for k in range(1, 8):
                t, dev = at_plane(k)
                c = remote(
                    gathered.at[it, yx, part], gathered.at[it, yx, part],
                    ag_send_sem.at[it, part, k], ag_recv_sem.at[it, part, k], dev,
                )
                c.start()
                sent.append(c)
            forwards.append(sent)
            if it == 0 and part == 0:
                prepare_covar(6, 8)

        smoothed = None
        for part in range(2):
            for k in range(8):
                if k:
                    forwards[part][k - 1].wait_recv()
                t = (yx - k + 8) % 8
                p = lax.dot_general(
                    gathered[it, t, part], covar[:, pl.ds(pl.multiple_of(512 * t + 256 * part, 256), 256)], NT,
                    preferred_element_type=F32,
                )
                smoothed = p if smoothed is None else smoothed + p
        if it == 0:
            for c in bounds:
                c.wait()
        edge = bound_recv[...].reshape(64, 128)
        lo = jnp.broadcast_to(edge[:, 0:1], (64, 512))
        hi = jnp.broadcast_to(edge[:, 64:65], (64, 512))
        now = start_recv[...].reshape(64, 512) if it == 0 else state[...]
        nxt = jnp.minimum(jnp.maximum(now - 0.02 * smoothed, lo), hi)
        if it < ITERS - 1:
            state[...] = nxt
        else:
            final_send[...] = nxt.reshape(8, 8, 512)
        for c in copies.values():
            c.wait_send()
        for sent in forwards:
            for c in sent:
                c.wait_send()

    copies = []
    for k in range(1, 8):
        t, dev = at_plane(k)
        c = remote(final_send.at[t], final_recv.at[yx], plane_send_sem.at[2, k], plane_recv_sem.at[2, k], dev)
        c.start()
        copies.append(c)
    final_recv[yx] = final_send[yx]
    for c in copies:
        c.wait()
    for h in range(2):
        for a in range(4):
            parts = [final_recv[4 * h + c, :, pl.ds(128 * a, 128)] for c in range(4)]
            for b, y in enumerate(swap_blocks(parts, quarter8)):
                out[:, pl.ds(128 * (2 * (4 * a + b) + h), 128)] = y


def per_device(gains, response, student, blocks, order, lower, upper, lengths, amplitude):
    hbm = pl.BlockSpec(memory_space=pltpu.HBM)
    return pl.pallas_call(
        kernel,
        out_shape=jax.ShapeDtypeStruct((8, 4096), F32),
        in_specs=[hbm] * 9,
        out_specs=pl.BlockSpec(memory_space=pltpu.VMEM),
        scratch_shapes=[
            pltpu.VMEM((8, 4096), F32),
            pltpu.SMEM((8,), F32),
            pltpu.SMEM((8,), F32),
            pltpu.VMEM((32, 1024), BF16),
            pltpu.VMEM((32, 1024), BF16),
            pltpu.VMEM((4, 256, 256), BF16),
            pltpu.VMEM((8, 128), jnp.int32),
            pltpu.VMEM((32, 128), F32),
            pltpu.VMEM((32, 128), F32),
            pltpu.VMEM((8, 8, 512), F32),
            pltpu.VMEM((8, 8, 512), F32),
            pltpu.VMEM((8, 128), F32),
            pltpu.VMEM((8, 8, 128), F32),
            pltpu.VMEM((64, 512), F32),
            pltpu.VMEM((16, 16, 128), BF16),
            pltpu.VMEM((ITERS, 16, 16, 128), BF16),
            pltpu.VMEM((16, 16, 128), BF16),
            pltpu.VMEM((ITERS, 16, 16, 128), BF16),
            pltpu.VMEM((ITERS, 8, 2, 64, 256), BF16),
            pltpu.VMEM((8, 8, 512), F32),
            pltpu.VMEM((8, 8, 512), F32),
            pltpu.VMEM((1024, 1024), BF16),
            pltpu.VMEM((1024, 1024), BF16),
            pltpu.VMEM((256, 128), F32),
            pltpu.VMEM((256, 128), F32),
            pltpu.VMEM((256, 1024), BF16),
            pltpu.VMEM((512, 4096), BF16),
            pltpu.VMEM((8, 512), F32),
            pltpu.VMEM((8, 512), F32),
            pltpu.VMEM((8, 512), F32),
            pltpu.VMEM((8, 512), F32),
            pltpu.VMEM((4, 128, 128), F32),
            pltpu.VMEM((4, 128, 128), F32),
            pltpu.VMEM((4, 128, 128), F32),
            pltpu.SemaphoreType.DMA((9,)),
            pltpu.SemaphoreType.REGULAR,
            pltpu.SemaphoreType.DMA((3, 8)),
            pltpu.SemaphoreType.DMA((3, 8)),
            pltpu.SemaphoreType.DMA((ITERS, 2, 8)),
            pltpu.SemaphoreType.DMA((ITERS, 2, 8)),
            pltpu.SemaphoreType.DMA((ITERS, 2, 16)),
            pltpu.SemaphoreType.DMA((ITERS, 2, 16)),
        ],
        compiler_params=pltpu.CompilerParams(collective_id=0, has_side_effects=True, vmem_limit_bytes=24 << 20),
        name="track",
    )(
        gains, lower, upper, response, student, blocks,
        order.reshape(8, 128), lengths.reshape(32, 128), amplitude.reshape(32, 128),
    )


def solution(mesh):
    placed = (
        P(("half", "wide"), None),
        P("wide", "half"),
        P("wide", "half"),
        P("half", None, None),
        P("half"),
        P(("half", "wide")),
        P(("half", "wide")),
        P(),
        P(),
    )
    return jax.shard_map(
        per_device, mesh=mesh, in_specs=placed, out_specs=P(("half", "wide"), None), check_vma=False
    )
```

```python
import functools

import jax
import jax.numpy as jnp
from jax import lax
from jax.experimental import pallas as pl
from jax.experimental.pallas import tpu as pltpu
from jax.sharding import PartitionSpec as P

ITERS = 2
F32 = jnp.float32
BF16 = jnp.bfloat16
NEAR = (-4, 4, -3, 3, -2, 2, -1, 1)
FAR = (8, 7, 9, 6, 10, 5, 11, 4)
CLOSE = (12, 3, 13, 2, 14, 1, 15)
PLANE = (5, 4, 3, 7, 2, 6, 1)
FROM = (0, 1, -2, -1, -4, -3, 2, 3, 4, 5, -6, -5, -8, -7, 6, 7)
NT = (((1,), (1,)), ((), ()))


def swap_blocks(parts, quarter):
    out = []
    for b in range(4):
        acc = None
        for g in range(4):
            moved = parts[g] if g == b else pltpu.roll(parts[g], (32 * (g - b)) % 128, 1)
            acc = moved if acc is None else jnp.where(quarter == g, moved, acc)
        out.append(acc)
    return out


def kernel(
    gains_hbm, lower_hbm, upper_hbm, response_hbm, student_hbm, blocks_hbm, order_hbm, lengths_hbm, amplitude_hbm,
    out,
    gains, lower, upper, response, student, blocks, order, lengths, amplitude,
    start_send, start_recv, bound_send, bound_recv, state,
    pack_send, pack_recv, mis_send, mis_recv, gathered, final_send, final_recv,
    onehot, matrix, moved, partial, tall, resp_tile, stud_tile, spread, covar, len_abs, amp_abs, len_rel, amp_rel, len_col, amp_col, pos_col,
    load_sem, entry_sem, plane_send_sem, plane_recv_sem, ag_send_sem, ag_recv_sem, col_send_sem, col_recv_sem,
):
    wide = lax.axis_index("wide")
    z = wide // 8
    yx = wide % 8

    def at_plane(k, sign=1):
        t = ((yx // 2 + sign * (k // 2) + 4) % 4) * 2 + (yx % 2 + k) % 2
        return t, {"wide": z * 8 + t}

    def at_column(k):
        t = (z + k + 16) % 16
        return t, {"wide": t * 8 + yx}

    def signal(sem, dev):
        pl.semaphore_signal(sem, inc=1, device_id=dev, device_id_type=pl.DeviceIdType.MESH)

    barrier = pltpu.get_barrier_semaphore()
    for k in NEAR:
        signal(barrier, at_column(k)[1])
    for k in PLANE:
        signal(barrier, at_plane(k)[1])

    loads = []
    for n, (src, dst) in enumerate((
        (gains_hbm, gains), (order_hbm, order), (blocks_hbm, blocks), (lower_hbm, lower), (upper_hbm, upper),
        (lengths_hbm, lengths), (amplitude_hbm, amplitude), (response_hbm, response), (student_hbm, student),
    )):
        c = pltpu.make_async_copy(src, dst, load_sem.at[n])
        c.start()
        loads.append(c)

    def remote(src, dst, ssem, rsem, dev):
        return pltpu.make_async_remote_copy(
            src_ref=src, dst_ref=dst, send_sem=ssem, recv_sem=rsem,
            device_id=dev, device_id_type=pl.DeviceIdType.MESH,
        )

    quarter8 = lax.broadcasted_iota(jnp.int32, (8, 128), 1) // 32
    quarter16 = lax.broadcasted_iota(jnp.int32, (16, 128), 1) // 32
    quarter128 = lax.broadcasted_iota(jnp.int32, (128, 128), 1) // 32

    loads[0].wait()
    for h in range(2):
        for a in range(4):
            parts = [gains[:, pl.ds(128 * (2 * (4 * a + b) + h), 128)] for b in range(4)]
            for c, y in enumerate(swap_blocks(parts, quarter8)):
                start_send[4 * h + c, :, pl.ds(128 * a, 128)] = y

    pl.semaphore_wait(barrier, 7 + len(NEAR))
    for k in (4, -4):
        signal(entry_sem, at_column(k)[1])

    starts = []
    for k in PLANE:
        t, dev = at_plane(k)
        c = remote(start_send.at[t], start_recv.at[yx], plane_send_sem.at[0, k], plane_recv_sem.at[0, k], dev)
        c.start()
        starts.append(c)
    start_recv[yx] = start_send[yx]

    loads[1].wait()
    row = lax.broadcasted_iota(jnp.int32, (1024, 128), 0)
    chan = ((z + 12 + (row // 512) * 8 + (row // 16) % 8) % 16) * 64 + ((row // 128) % 4) * 16 + row % 16
    for j in range(8):
        onehot[:, pl.ds(128 * j, 128)] = jnp.where(chan == order[pl.ds(j, 1), :], 1.0, 0.0).astype(BF16)
    loads[2].wait()

    @pl.loop(0, 4)
    def _(q):
        rows = pl.ds(pl.multiple_of(q * 256, 256), 256)
        for b in range(4):
            spread[:, pl.ds(256 * b, 256)] = jnp.dot(
                onehot[rows, pl.ds(256 * b, 256)], blocks[b], preferred_element_type=F32
            ).astype(BF16)
        matrix[rows, :] = lax.dot_general(
            spread[...], onehot[...], NT, preferred_element_type=F32
        ).astype(BF16)

    for c in starts:
        c.wait()
    pl.semaphore_wait(entry_sem, 2)

    def send_column(copies, ks, it, which, send, at_send, recv, at_recv):
        for k in ks:
            t, dev = at_column(k)
            c = remote(
                send.at[at_send(k)], recv.at[it, at_recv(k)],
                col_send_sem.at[it, which, k], col_recv_sem.at[it, which, k], dev,
            )
            c.start()
            copies[k] = c

    def send_bounds():
        loads[3].wait()
        loads[4].wait()
        i0 = lax.broadcasted_iota(jnp.int32, (8, 128), 0)
        left = lax.broadcasted_iota(jnp.int32, (8, 128), 1) < 64
        tile = jnp.zeros((8, 128), F32)
        for r in range(8):
            tile = jnp.where(i0 == r, jnp.where(left, lower[r], upper[r]), tile)
        bound_send[...] = tile
        copies = []
        for k in PLANE:
            _, dev = at_plane(k)
            c = remote(bound_send, bound_recv.at[yx], plane_send_sem.at[1, k], plane_recv_sem.at[1, k], dev)
            c.start()
            copies.append(c)
        bound_recv[yx] = tile
        return copies

    def prepare_rest():
        loads[7].wait()
        loads[8].wait()
        for src, dst in ((response, resp_tile), (student, stud_tile)):
            x = src[...].astype(F32)
            tall[...] = jnp.transpose(jnp.concatenate([x, x, x, x], axis=0))
            for s in range(16):
                first = ((z + 12 + s) % 16) * 64
                acc = tall[pl.ds(pl.multiple_of(first, 64), 16), :]
                for g in range(1, 4):
                    acc = jnp.where(quarter16 == g, tall[pl.ds(pl.multiple_of(first + 16 * g, 16), 16), :], acc)
                dst[pl.ds(16 * s, 16), :] = acc

    def by_slot(x):
        v = [x[:, 128 * n : 128 * n + 128] for n in range(4)]
        left = lax.broadcasted_iota(jnp.int32, v[0].shape, 1) < 64
        return jnp.concatenate(
            [jnp.where(left, v[a], v[b]) for a, b in ((2, 1), (1, 2), (3, 0), (0, 3))], axis=1
        )

    def prepare_rows():
        loads[5].wait()
        loads[6].wait()
        quarter1 = lax.broadcasted_iota(jnp.int32, (1, 128), 1) // 32
        for src, dst in ((lengths, len_abs), (amplitude, amp_abs)):
            for h in range(2):
                for a in range(4):
                    parts = [src[pl.ds(h + 2 * b + 8 * a, 1), :] for b in range(4)]
                    for c, y in enumerate(swap_blocks(parts, quarter1)):
                        dst[pl.ds(4 * h + c, 1), pl.ds(128 * a, 128)] = y
        turn = ((24 - z) % 16) * 32
        len_all = len_abs[...]
        amp_all = amp_abs[...] * jnp.sqrt(len_all)
        len_rel[...] = by_slot(pltpu.roll(len_all * len_all, turn, 1))
        amp_rel[...] = by_slot(pltpu.roll(amp_all, turn, 1))
        own_len = len_abs[pl.ds(yx, 1), :]
        own_amp = amp_abs[pl.ds(yx, 1), :]
        i0 = lax.broadcasted_iota(jnp.int32, (128, 128), 0)
        for a in range(4):
            lc = jnp.transpose(jnp.broadcast_to(own_len[:, 128 * a : 128 * a + 128], (128, 128)))
            ac = jnp.transpose(jnp.broadcast_to(own_amp[:, 128 * a : 128 * a + 128], (128, 128)))
            len_col[a] = lc * lc
            amp_col[a] = ac * jnp.sqrt(2.0 * lc)
            pos_col[a] = ((4 * a + i0 // 32) * 256 + i0 % 32 + yx * 32).astype(F32)

    def prepare_covar(first, last):
        i1 = lax.broadcasted_iota(jnp.int32, (1, 512), 1)
        pos = by_slot((((i1 // 32 + z + 8) % 16) * 256 + i1 % 32).astype(F32))

        @pl.loop(first, last)
        def _(t):
            lrow = len_rel[pl.ds(t, 1), :]
            arow = amp_rel[pl.ds(t, 1), :]
            prow = pos + (t * 32).astype(F32)
            for b in range(4):
                lr = lrow[:, 128 * b : 128 * b + 128]
                ar = arow[:, 128 * b : 128 * b + 128]
                pr = prow[:, 128 * b : 128 * b + 128]
                for a in range(4):
                    inv = lax.rsqrt(len_col[a] + lr)
                    q = (pos_col[a] - pr) * inv
                    vals = (amp_col[a] * ar) * (inv * jnp.exp(-(q * q)))
                    covar[pl.ds(128 * a, 128), pl.ds(pl.multiple_of(512 * t + 128 * b, 128), 128)] = vals.astype(BF16)

    def plane_of(k):
        return (z + k) % 16

    def order_of(k):
        return (k + 4) % 16

    def order_from(k):
        return (4 - k) % 16

    def slot_of_piece(k):
        return FROM.index((8 - k) % 16 - 8)

    for it in range(ITERS):
        now = start_recv[...].reshape(64, 512) if it == 0 else state[...]
        for a in range(4):
            parts = [now[16 * g : 16 * g + 16, 128 * a : 128 * a + 128] for g in range(4)]
            for b, y in enumerate(swap_blocks(parts, quarter16)):
                pack_send[4 * a + b] = y.astype(BF16)
        copies = {}
        send_column(copies, FAR + CLOSE, it, 0, pack_send, plane_of, pack_recv, order_from)
        pack_recv[it, 4] = pack_send[z]
        if it == 0:
            bounds = send_bounds()
            prepare_rest()
            prepare_rows()
            prepare_covar(0, 4)

        def take(half):
            got = pack_recv[it, pl.ds(8 * half, 8)].astype(F32).reshape(128, 128)
            for g in range(4):
                x = jnp.where(quarter128 == g, got, 0.0)
                x = x + pltpu.roll(x, 32, 1)
                x = x + pltpu.roll(x, 64, 1)
                moved[pl.ds(512 * half + 128 * g, 128), :] = x.astype(BF16)

        for k, c in copies.items():
            if order_from(k) < 8:
                c.wait_recv()
        take(0)
        partial[...] = jnp.dot(matrix[:, pl.ds(0, 512)], moved[pl.ds(0, 512), :], preferred_element_type=F32)
        for k, c in copies.items():
            if order_from(k) >= 8:
                c.wait_recv()
        take(1)
        for c in copies.values():
            c.wait_send()
        copies = {}
        for half, ks in ((1, FAR), (0, CLOSE)):
            rows = pl.ds(512 * half, 512)
            full = partial[rows, :] + jnp.dot(
                matrix[rows, pl.ds(512, 512)], moved[pl.ds(512, 512), :], preferred_element_type=F32
            )
            prod = full[0:128]
            for g in range(1, 4):
                prod = jnp.where(quarter128 == g, full[128 * g : 128 * g + 128], prod)
            own = pl.ds(128 * half, 128)
            misfit = (stud_tile[own, :] * (prod - resp_tile[own, :])).astype(BF16)
            mis_send[pl.ds(8 * half, 8)] = misfit.reshape(8, 16, 128)
            send_column(copies, ks, it, 1, mis_send, order_of, mis_recv, slot_of_piece)
        mis_recv[it, slot_of_piece(0)] = mis_send[4]
        if it == 0:
            prepare_covar(4, 6)

        forwards = []
        for part in range(4):
            for k, c in copies.items():
                if slot_of_piece(k) // 4 == part:
                    c.wait_recv()
            parts = [mis_recv[it, 4 * part + b].astype(F32) for b in range(4)]
            for g, y in enumerate(swap_blocks(parts, quarter16)):
                gathered[it, yx, part, pl.ds(16 * g, 16), :] = y.astype(BF16)
            sent = []
            for k in PLANE:
                t, dev = at_plane(k)
                c = remote(
                    gathered.at[it, yx, part], gathered.at[it, yx, part],
                    ag_send_sem.at[it, part, k], ag_recv_sem.at[it, part, k], dev,
                )
                c.start()
                sent.append(c)
            forwards.append(sent)
            if it == 0 and part == 1:
                prepare_covar(6, 7)
        if it == 0:
            prepare_covar(7, 8)

        smoothed = None
        for parts in ((0, 1), (2,), (3,)):
            for n in range(0, 8, 3 - len(parts)):
                left, right = [], []
                for m in range(n, n + 3 - len(parts)):
                    t = at_plane(PLANE[-m], -1)[0] if m else yx
                    for part in parts:
                        if m:
                            forwards[part][-m].wait_recv()
                        left.append(gathered[it, t, part])
                        right.append(covar[:, pl.ds(pl.multiple_of(512 * t + 128 * part, 128), 128)])
                p = lax.dot_general(
                    jnp.concatenate(left, axis=1), jnp.concatenate(right, axis=1), NT, preferred_element_type=F32
                )
                smoothed = p if smoothed is None else smoothed + p
        if it == 0:
            for c in bounds:
                c.wait()
        edge = bound_recv[...].reshape(64, 128)
        lo = jnp.broadcast_to(edge[:, 0:1], (64, 512))
        hi = jnp.broadcast_to(edge[:, 64:65], (64, 512))
        now = start_recv[...].reshape(64, 512) if it == 0 else state[...]
        nxt = jnp.minimum(jnp.maximum(now - 0.02 * smoothed, lo), hi)
        if it < ITERS - 1:
            state[...] = nxt
        else:
            final_send[...] = nxt.reshape(8, 8, 512)
        for c in copies.values():
            c.wait_send()
        for sent in forwards:
            for c in sent:
                c.wait_send()

    copies = []
    for k in PLANE:
        t, dev = at_plane(k)
        c = remote(final_send.at[t], final_recv.at[yx], plane_send_sem.at[2, k], plane_recv_sem.at[2, k], dev)
        c.start()
        copies.append(c)
    final_recv[yx] = final_send[yx]
    for c in copies:
        c.wait()
    for h in range(2):
        for a in range(4):
            parts = [final_recv[4 * h + c, :, pl.ds(128 * a, 128)] for c in range(4)]
            for b, y in enumerate(swap_blocks(parts, quarter8)):
                out[:, pl.ds(128 * (2 * (4 * a + b) + h), 128)] = y


def per_device(gains, response, student, blocks, order, lower, upper, lengths, amplitude):
    hbm = pl.BlockSpec(memory_space=pltpu.HBM)
    return pl.pallas_call(
        kernel,
        out_shape=jax.ShapeDtypeStruct((8, 4096), F32),
        in_specs=[hbm] * 9,
        out_specs=pl.BlockSpec(memory_space=pltpu.VMEM),
        scratch_shapes=[
            pltpu.VMEM((8, 4096), F32),
            pltpu.SMEM((8,), F32),
            pltpu.SMEM((8,), F32),
            pltpu.VMEM((32, 1024), BF16),
            pltpu.VMEM((32, 1024), BF16),
            pltpu.VMEM((4, 256, 256), BF16),
            pltpu.VMEM((8, 128), jnp.int32),
            pltpu.VMEM((32, 128), F32),
            pltpu.VMEM((32, 128), F32),
            pltpu.VMEM((8, 8, 512), F32),
            pltpu.VMEM((8, 8, 512), F32),
            pltpu.VMEM((8, 128), F32),
            pltpu.VMEM((8, 8, 128), F32),
            pltpu.VMEM((64, 512), F32),
            pltpu.VMEM((16, 16, 128), BF16),
            pltpu.VMEM((ITERS, 16, 16, 128), BF16),
            pltpu.VMEM((16, 16, 128), BF16),
            pltpu.VMEM((ITERS, 16, 16, 128), BF16),
            pltpu.VMEM((ITERS, 8, 4, 64, 128), BF16),
            pltpu.VMEM((8, 8, 512), F32),
            pltpu.VMEM((8, 8, 512), F32),
            pltpu.VMEM((1024, 1024), BF16),
            pltpu.VMEM((1024, 1024), BF16),
            pltpu.VMEM((1024, 128), BF16),
            pltpu.VMEM((1024, 128), F32),
            pltpu.VMEM((1024, 128), F32),
            pltpu.VMEM((256, 128), F32),
            pltpu.VMEM((256, 128), F32),
            pltpu.VMEM((256, 1024), BF16),
            pltpu.VMEM((512, 4096), BF16),
            pltpu.VMEM((8, 512), F32),
            pltpu.VMEM((8, 512), F32),
            pltpu.VMEM((8, 512), F32),
            pltpu.VMEM((8, 512), F32),
            pltpu.VMEM((4, 128, 128), F32),
            pltpu.VMEM((4, 128, 128), F32),
            pltpu.VMEM((4, 128, 128), F32),
            pltpu.SemaphoreType.DMA((9,)),
            pltpu.SemaphoreType.REGULAR,
            pltpu.SemaphoreType.DMA((3, 8)),
            pltpu.SemaphoreType.DMA((3, 8)),
            pltpu.SemaphoreType.DMA((ITERS, 4, 8)),
            pltpu.SemaphoreType.DMA((ITERS, 4, 8)),
            pltpu.SemaphoreType.DMA((ITERS, 2, 16)),
            pltpu.SemaphoreType.DMA((ITERS, 2, 16)),
        ],
        compiler_params=pltpu.CompilerParams(collective_id=0, has_side_effects=True, vmem_limit_bytes=24 << 20),
        name="track",
    )(*[
        pltpu.with_memory_space_constraint(v, pltpu.HBM)
        for v in (
            gains, lower, upper, response, student, blocks,
            order.reshape(8, 128), lengths.reshape(32, 128), amplitude.reshape(32, 128),
        )
    ])


def solution(mesh):
    placed = (
        P(("half", "wide"), None),
        P("wide", "half"),
        P("wide", "half"),
        P("half", None, None),
        P("half"),
        P(("half", "wide")),
        P(("half", "wide")),
        P(),
        P(),
    )
    return jax.shard_map(
        per_device, mesh=mesh, in_specs=placed, out_specs=P(("half", "wide"), None), check_vma=False
    )
```

```python
import functools

import jax
import jax.numpy as jnp
from jax import lax
from jax.experimental import pallas as pl
from jax.experimental.pallas import tpu as pltpu
from jax.sharding import PartitionSpec as P

ITERS = 2
F32 = jnp.float32
BF16 = jnp.bfloat16
NEAR = (-4, 4, -3, 3, -2, 2, -1, 1)
FAR = (8, 7, 9, 6, 10, 5, 11, 4)
CLOSE = (12, 3, 13, 2, 14, 1, 15)
PLANE = (5, 4, 3, 7, 2, 6, 1)
FROM = (0, 1, -2, -1, -4, -3, 2, 3, 4, 5, -6, -5, -8, -7, 6, 7)
NT = (((1,), (1,)), ((), ()))


def swap_blocks(parts, quarter):
    out = []
    for b in range(4):
        acc = None
        for g in range(4):
            moved = parts[g] if g == b else pltpu.roll(parts[g], (32 * (g - b)) % 128, 1)
            acc = moved if acc is None else jnp.where(quarter == g, moved, acc)
        out.append(acc)
    return out


def kernel(
    gains_hbm, lower_hbm, upper_hbm, response_hbm, student_hbm, blocks_hbm, order_hbm, lengths_hbm, amplitude_hbm,
    out,
    gains, lower, upper, response, student, blocks, order, lengths, amplitude,
    start_send, start_recv, bound_send, bound_recv, state,
    pack_send, pack_recv, mis_send, mis_recv, gathered, final_send, final_recv,
    onehot, matrix, moved, partial, tall, resp_tile, stud_tile, spread, covar, len_abs, amp_abs, own_row, len_col, amp_col, pos_col,
    load_sem, entry_sem, plane_send_sem, plane_recv_sem, ag_send_sem, ag_recv_sem, col_send_sem, col_recv_sem,
):
    wide = lax.axis_index("wide")
    z = wide // 8
    yx = wide % 8

    def at_plane(k, sign=1):
        t = ((yx // 2 + sign * (k // 2) + 4) % 4) * 2 + (yx % 2 + k) % 2
        return t, {"wide": z * 8 + t}

    def at_column(k):
        t = (z + k + 16) % 16
        return t, {"wide": t * 8 + yx}

    def signal(sem, dev):
        pl.semaphore_signal(sem, inc=1, device_id=dev, device_id_type=pl.DeviceIdType.MESH)

    barrier = pltpu.get_barrier_semaphore()
    for k in NEAR:
        signal(barrier, at_column(k)[1])
    for k in PLANE:
        signal(barrier, at_plane(k)[1])

    loads = []
    for n, (src, dst) in enumerate((
        (gains_hbm, gains), (order_hbm, order), (blocks_hbm, blocks), (lower_hbm, lower), (upper_hbm, upper),
        (lengths_hbm, lengths), (amplitude_hbm, amplitude), (response_hbm, response), (student_hbm, student),
    )):
        c = pltpu.make_async_copy(src, dst, load_sem.at[n])
        c.start()
        loads.append(c)

    def remote(src, dst, ssem, rsem, dev):
        return pltpu.make_async_remote_copy(
            src_ref=src, dst_ref=dst, send_sem=ssem, recv_sem=rsem,
            device_id=dev, device_id_type=pl.DeviceIdType.MESH,
        )

    quarter8 = lax.broadcasted_iota(jnp.int32, (8, 128), 1) // 32
    quarter16 = lax.broadcasted_iota(jnp.int32, (16, 128), 1) // 32
    quarter128 = lax.broadcasted_iota(jnp.int32, (128, 128), 1) // 32

    loads[0].wait()
    for h in range(2):
        for a in range(4):
            parts = [gains[:, pl.ds(128 * (2 * (4 * a + b) + h), 128)] for b in range(4)]
            for c, y in enumerate(swap_blocks(parts, quarter8)):
                start_send[4 * h + c, :, pl.ds(128 * a, 128)] = y

    pl.semaphore_wait(barrier, 7 + len(NEAR))
    for k in (4, -4):
        signal(entry_sem, at_column(k)[1])

    starts = []
    for k in PLANE:
        t, dev = at_plane(k)
        c = remote(start_send.at[t], start_recv.at[yx], plane_send_sem.at[0, k], plane_recv_sem.at[0, k], dev)
        c.start()
        starts.append(c)
    start_recv[yx] = start_send[yx]

    loads[1].wait()
    row = lax.broadcasted_iota(jnp.int32, (1024, 128), 0)
    chan = ((z + 12 + (row // 512) * 8 + (row // 16) % 8) % 16) * 64 + ((row // 128) % 4) * 16 + row % 16
    for j in range(8):
        onehot[:, pl.ds(128 * j, 128)] = jnp.where(chan == order[pl.ds(j, 1), :], 1.0, 0.0).astype(BF16)
    loads[2].wait()

    @pl.loop(0, 4)
    def _(q):
        rows = pl.ds(pl.multiple_of(q * 256, 256), 256)
        for b in range(4):
            spread[:, pl.ds(256 * b, 256)] = jnp.dot(
                onehot[rows, pl.ds(256 * b, 256)], blocks[b], preferred_element_type=F32
            ).astype(BF16)
        matrix[rows, :] = lax.dot_general(
            spread[...], onehot[...], NT, preferred_element_type=F32
        ).astype(BF16)

    for c in starts:
        c.wait()
    pl.semaphore_wait(entry_sem, 2)

    def send_column(copies, ks, it, which, send, at_send, recv, at_recv):
        for k in ks:
            t, dev = at_column(k)
            c = remote(
                send.at[at_send(k)], recv.at[it, at_recv(k)],
                col_send_sem.at[it, which, k], col_recv_sem.at[it, which, k], dev,
            )
            c.start()
            copies[k] = c

    def send_bounds():
        loads[3].wait()
        loads[4].wait()
        i0 = lax.broadcasted_iota(jnp.int32, (8, 128), 0)
        left = lax.broadcasted_iota(jnp.int32, (8, 128), 1) < 64
        tile = jnp.zeros((8, 128), F32)
        for r in range(8):
            tile = jnp.where(i0 == r, jnp.where(left, lower[r], upper[r]), tile)
        bound_send[...] = tile
        copies = []
        for k in PLANE:
            _, dev = at_plane(k)
            c = remote(bound_send, bound_recv.at[yx], plane_send_sem.at[1, k], plane_recv_sem.at[1, k], dev)
            c.start()
            copies.append(c)
        bound_recv[yx] = tile
        return copies

    def prepare_rest():
        loads[7].wait()
        loads[8].wait()
        for src, dst in ((response, resp_tile), (student, stud_tile)):
            x = src[...].astype(F32)
            tall[...] = jnp.transpose(jnp.concatenate([x, x, x, x], axis=0))
            for s in range(16):
                first = ((z + 12 + s) % 16) * 64
                acc = tall[pl.ds(pl.multiple_of(first, 64), 16), :]
                for g in range(1, 4):
                    acc = jnp.where(quarter16 == g, tall[pl.ds(pl.multiple_of(first + 16 * g, 16), 16), :], acc)
                dst[pl.ds(16 * s, 16), :] = acc

    def by_slot(x):
        v = [x[:, 128 * n : 128 * n + 128] for n in range(4)]
        left = lax.broadcasted_iota(jnp.int32, v[0].shape, 1) < 64
        return jnp.concatenate(
            [jnp.where(left, v[a], v[b]) for a, b in ((2, 1), (1, 2), (3, 0), (0, 3))], axis=1
        )

    def prepare_rows():
        loads[5].wait()
        loads[6].wait()
        quarter1 = lax.broadcasted_iota(jnp.int32, (1, 128), 1) // 32
        for src, dst in ((lengths, len_abs), (amplitude, amp_abs)):
            for h in range(2):
                for a in range(4):
                    parts = [src[pl.ds(h + 2 * b + 8 * a, 1), :] for b in range(4)]
                    for c, y in enumerate(swap_blocks(parts, quarter1)):
                        dst[pl.ds(4 * h + c, 1), pl.ds(128 * a, 128)] = y
        turn = ((24 - z) % 16) * 32
        len_all = len_abs[...]
        amp_all = amp_abs[...] * jnp.sqrt(len_all)
        i1 = lax.broadcasted_iota(jnp.int32, (8, 512), 1)
        sq = by_slot(pltpu.roll(len_all * len_all, turn, 1))
        am = by_slot(pltpu.roll(amp_all, turn, 1))
        ps = by_slot((((i1 // 32 + z + 8) % 16) * 256 + i1 % 32).astype(F32))
        for b in range(4):
            part = slice(128 * b, 128 * b + 128)
            sq_t, am_t, ps_t = jnp.transpose(sq[:, part]), jnp.transpose(am[:, part]), jnp.transpose(ps[:, part])
            pos_col[b] = jnp.broadcast_to(ps_t[:, 0:1], (128, 128))
            for t in range(8):
                len_col[t, b] = jnp.broadcast_to(sq_t[:, t : t + 1], (128, 128))
                amp_col[t, b] = jnp.broadcast_to(am_t[:, t : t + 1], (128, 128))
        own_len = len_abs[pl.ds(yx, 1), :]
        own_amp = amp_abs[pl.ds(yx, 1), :]
        own_row[pl.ds(0, 1), :] = own_len * own_len
        own_row[pl.ds(1, 1), :] = own_amp * jnp.sqrt(2.0 * own_len)
        own_row[pl.ds(2, 1), :] = ((i1 // 32) * 256 + i1 % 32 + yx * 32)[0:1].astype(F32)

    def prepare_covar(first, last):
        @pl.loop(first, last)
        def _(t):
            shift = (t * 32).astype(F32)
            for b in range(4):
                rows = pl.ds(pl.multiple_of(512 * t + 128 * b, 128), 128)
                for a in range(4):
                    part = pl.ds(128 * a, 128)
                    inv = lax.rsqrt(len_col[t, b] + own_row[pl.ds(0, 1), part])
                    q = (pos_col[b] - (own_row[pl.ds(2, 1), part] - shift)) * inv
                    vals = (amp_col[t, b] * own_row[pl.ds(1, 1), part]) * (inv * jnp.exp(-(q * q)))
                    covar[rows, part] = vals.astype(BF16)

    def plane_of(k):
        return (z + k) % 16

    def order_of(k):
        return (k + 4) % 16

    def order_from(k):
        return (4 - k) % 16

    def slot_of_piece(k):
        return FROM.index((8 - k) % 16 - 8)

    for it in range(ITERS):
        now = start_recv[...].reshape(64, 512) if it == 0 else state[...]
        for a in range(4):
            parts = [now[16 * g : 16 * g + 16, 128 * a : 128 * a + 128] for g in range(4)]
            for b, y in enumerate(swap_blocks(parts, quarter16)):
                pack_send[4 * a + b] = y.astype(BF16)
        copies = {}
        send_column(copies, FAR + CLOSE, it, 0, pack_send, plane_of, pack_recv, order_from)
        pack_recv[it, 4] = pack_send[z]
        if it == 0:
            bounds = send_bounds()
            prepare_rest()
            prepare_rows()
            prepare_covar(0, 3)

        def take(half):
            got = pack_recv[it, pl.ds(8 * half, 8)].astype(F32).reshape(128, 128)
            for g in range(4):
                x = jnp.where(quarter128 == g, got, 0.0)
                x = x + pltpu.roll(x, 32, 1)
                x = x + pltpu.roll(x, 64, 1)
                moved[pl.ds(512 * half + 128 * g, 128), :] = x.astype(BF16)

        for k, c in copies.items():
            if order_from(k) < 8:
                c.wait_recv()
        take(0)
        partial[...] = jnp.dot(matrix[:, pl.ds(0, 512)], moved[pl.ds(0, 512), :], preferred_element_type=F32)
        for k, c in copies.items():
            if order_from(k) >= 8:
                c.wait_recv()
        take(1)
        for c in copies.values():
            c.wait_send()
        copies = {}
        for half, ks in ((1, FAR), (0, CLOSE)):
            rows = pl.ds(512 * half, 512)
            full = partial[rows, :] + jnp.dot(
                matrix[rows, pl.ds(512, 512)], moved[pl.ds(512, 512), :], preferred_element_type=F32
            )
            prod = full[0:128]
            for g in range(1, 4):
                prod = jnp.where(quarter128 == g, full[128 * g : 128 * g + 128], prod)
            own = pl.ds(128 * half, 128)
            misfit = (stud_tile[own, :] * (prod - resp_tile[own, :])).astype(BF16)
            mis_send[pl.ds(8 * half, 8)] = misfit.reshape(8, 16, 128)
            send_column(copies, ks, it, 1, mis_send, order_of, mis_recv, slot_of_piece)
        mis_recv[it, slot_of_piece(0)] = mis_send[4]
        if it == 0:
            prepare_covar(3, 5)

        forwards = []
        for part in range(4):
            for k, c in copies.items():
                if slot_of_piece(k) // 4 == part:
                    c.wait_recv()
            parts = [mis_recv[it, 4 * part + b].astype(F32) for b in range(4)]
            for g, y in enumerate(swap_blocks(parts, quarter16)):
                gathered[it, yx, part, pl.ds(16 * g, 16), :] = y.astype(BF16)
            sent = []
            for k in PLANE:
                t, dev = at_plane(k)
                c = remote(
                    gathered.at[it, yx, part], gathered.at[it, yx, part],
                    ag_send_sem.at[it, part, k], ag_recv_sem.at[it, part, k], dev,
                )
                c.start()
                sent.append(c)
            forwards.append(sent)
            if it == 0 and part == 1:
                prepare_covar(5, 6)
        if it == 0:
            prepare_covar(6, 8)

        smoothed = None
        for parts in ((0, 1), (2,), (3,)):
            for n in range(0, 8, 3 - len(parts)):
                left, right = [], []
                for m in range(n, n + 3 - len(parts)):
                    t = at_plane(PLANE[-m], -1)[0] if m else yx
                    for part in parts:
                        if m:
                            forwards[part][-m].wait_recv()
                        left.append(gathered[it, t, part])
                        right.append(covar[pl.ds(pl.multiple_of(512 * t + 128 * part, 128), 128), :])
                p = jnp.dot(
                    jnp.concatenate(left, axis=1), jnp.concatenate(right, axis=0), preferred_element_type=F32
                )
                smoothed = p if smoothed is None else smoothed + p
        if it == 0:
            for c in bounds:
                c.wait()
        edge = bound_recv[...].reshape(64, 128)
        lo = jnp.broadcast_to(edge[:, 0:1], (64, 512))
        hi = jnp.broadcast_to(edge[:, 64:65], (64, 512))
        now = start_recv[...].reshape(64, 512) if it == 0 else state[...]
        nxt = jnp.minimum(jnp.maximum(now - 0.02 * smoothed, lo), hi)
        if it < ITERS - 1:
            state[...] = nxt
        else:
            final_send[...] = nxt.reshape(8, 8, 512)
        for c in copies.values():
            c.wait_send()
        for sent in forwards:
            for c in sent:
                c.wait_send()

    copies = []
    for k in PLANE:
        t, dev = at_plane(k)
        c = remote(final_send.at[t], final_recv.at[yx], plane_send_sem.at[2, k], plane_recv_sem.at[2, k], dev)
        c.start()
        copies.append(c)
    final_recv[yx] = final_send[yx]
    for c in copies:
        c.wait()
    for h in range(2):
        for a in range(4):
            parts = [final_recv[4 * h + c, :, pl.ds(128 * a, 128)] for c in range(4)]
            for b, y in enumerate(swap_blocks(parts, quarter8)):
                out[:, pl.ds(128 * (2 * (4 * a + b) + h), 128)] = y


def per_device(gains, response, student, blocks, order, lower, upper, lengths, amplitude):
    hbm = pl.BlockSpec(memory_space=pltpu.HBM)
    return pl.pallas_call(
        kernel,
        out_shape=jax.ShapeDtypeStruct((8, 4096), F32),
        in_specs=[hbm] * 9,
        out_specs=pl.BlockSpec(memory_space=pltpu.VMEM),
        scratch_shapes=[
            pltpu.VMEM((8, 4096), F32),
            pltpu.SMEM((8,), F32),
            pltpu.SMEM((8,), F32),
            pltpu.VMEM((32, 1024), BF16),
            pltpu.VMEM((32, 1024), BF16),
            pltpu.VMEM((4, 256, 256), BF16),
            pltpu.VMEM((8, 128), jnp.int32),
            pltpu.VMEM((32, 128), F32),
            pltpu.VMEM((32, 128), F32),
            pltpu.VMEM((8, 8, 512), F32),
            pltpu.VMEM((8, 8, 512), F32),
            pltpu.VMEM((8, 128), F32),
            pltpu.VMEM((8, 8, 128), F32),
            pltpu.VMEM((64, 512), F32),
            pltpu.VMEM((16, 16, 128), BF16),
            pltpu.VMEM((ITERS, 16, 16, 128), BF16),
            pltpu.VMEM((16, 16, 128), BF16),
            pltpu.VMEM((ITERS, 16, 16, 128), BF16),
            pltpu.VMEM((ITERS, 8, 4, 64, 128), BF16),
            pltpu.VMEM((8, 8, 512), F32),
            pltpu.VMEM((8, 8, 512), F32),
            pltpu.VMEM((1024, 1024), BF16),
            pltpu.VMEM((1024, 1024), BF16),
            pltpu.VMEM((1024, 128), BF16),
            pltpu.VMEM((1024, 128), F32),
            pltpu.VMEM((1024, 128), F32),
            pltpu.VMEM((256, 128), F32),
            pltpu.VMEM((256, 128), F32),
            pltpu.VMEM((256, 1024), BF16),
            pltpu.VMEM((4096, 512), BF16),
            pltpu.VMEM((8, 512), F32),
            pltpu.VMEM((8, 512), F32),
            pltpu.VMEM((8, 512), F32),
            pltpu.VMEM((8, 4, 128, 128), F32),
            pltpu.VMEM((8, 4, 128, 128), F32),
            pltpu.VMEM((4, 128, 128), F32),
            pltpu.SemaphoreType.DMA((9,)),
            pltpu.SemaphoreType.REGULAR,
            pltpu.SemaphoreType.DMA((3, 8)),
            pltpu.SemaphoreType.DMA((3, 8)),
            pltpu.SemaphoreType.DMA((ITERS, 4, 8)),
            pltpu.SemaphoreType.DMA((ITERS, 4, 8)),
            pltpu.SemaphoreType.DMA((ITERS, 2, 16)),
            pltpu.SemaphoreType.DMA((ITERS, 2, 16)),
        ],
        compiler_params=pltpu.CompilerParams(collective_id=0, has_side_effects=True, vmem_limit_bytes=24 << 20),
        name="track",
    )(*[
        pltpu.with_memory_space_constraint(v, pltpu.HBM)
        for v in (
            gains, lower, upper, response, student, blocks,
            order.reshape(8, 128), lengths.reshape(32, 128), amplitude.reshape(32, 128),
        )
    ])


def solution(mesh):
    placed = (
        P(("half", "wide"), None),
        P("wide", "half"),
        P("wide", "half"),
        P("half", None, None),
        P("half"),
        P(("half", "wide")),
        P(("half", "wide")),
        P(),
        P(),
    )
    return jax.shard_map(
        per_device, mesh=mesh, in_specs=placed, out_specs=P(("half", "wide"), None), check_vma=False
    )
```

```python
import functools

import jax
import jax.numpy as jnp
from jax import lax
from jax.experimental import pallas as pl
from jax.experimental.pallas import tpu as pltpu
from jax.sharding import PartitionSpec as P

ITERS = 2
F32 = jnp.float32
BF16 = jnp.bfloat16
NEAR = (-4, 4, -3, 3, -2, 2, -1, 1)
FAR = (8, 7, 9, 6, 10, 5, 11, 4)
CLOSE = (12, 3, 13, 2, 14, 1, 15)
PLANE = (5, 4, 3, 7, 2, 6, 1)
FROM = (0, 1, -2, -1, -4, -3, 2, 3, 4, 5, -6, -5, -8, -7, 6, 7)
NT = (((1,), (1,)), ((), ()))


def swap_blocks(parts, quarter):
    out = []
    for b in range(4):
        acc = None
        for g in range(4):
            moved = parts[g] if g == b else pltpu.roll(parts[g], (32 * (g - b)) % 128, 1)
            acc = moved if acc is None else jnp.where(quarter == g, moved, acc)
        out.append(acc)
    return out


def kernel(
    gains_hbm, lower_hbm, upper_hbm, response_hbm, student_hbm, blocks_hbm, order_hbm, lengths_hbm, amplitude_hbm,
    out,
    gains, lower, upper, response, student, blocks, order, lengths, amplitude,
    start_send, start_recv, bound_send, bound_recv, state,
    pack_send, pack_recv, mis_send, mis_recv, gathered, final_send, final_recv,
    onehot, matrix, moved, partial, tall, resp_tile, stud_tile, spread, covar, len_abs, amp_abs, own_row, len_col, amp_col, pos_col,
    load_sem, entry_sem, plane_send_sem, plane_recv_sem, ag_send_sem, ag_recv_sem, col_send_sem, col_recv_sem,
):
    wide = lax.axis_index("wide")
    z = wide // 8
    yx = wide % 8

    def at_plane(k, sign=1):
        t = ((yx // 2 + sign * (k // 2) + 4) % 4) * 2 + (yx % 2 + k) % 2
        return t, {"wide": z * 8 + t}

    def at_column(k):
        t = (z + k + 16) % 16
        return t, {"wide": t * 8 + yx}

    def signal(sem, dev):
        pl.semaphore_signal(sem, inc=1, device_id=dev, device_id_type=pl.DeviceIdType.MESH)

    barrier = pltpu.get_barrier_semaphore()
    for k in NEAR:
        signal(barrier, at_column(k)[1])
    for k in PLANE:
        signal(barrier, at_plane(k)[1])

    loads = []
    for n, (src, dst) in enumerate((
        (gains_hbm, gains), (order_hbm, order), (blocks_hbm, blocks), (lower_hbm, lower), (upper_hbm, upper),
        (lengths_hbm, lengths), (amplitude_hbm, amplitude), (response_hbm, response), (student_hbm, student),
    )):
        c = pltpu.make_async_copy(src, dst, load_sem.at[n])
        c.start()
        loads.append(c)

    def remote(src, dst, ssem, rsem, dev):
        return pltpu.make_async_remote_copy(
            src_ref=src, dst_ref=dst, send_sem=ssem, recv_sem=rsem,
            device_id=dev, device_id_type=pl.DeviceIdType.MESH,
        )

    quarter8 = lax.broadcasted_iota(jnp.int32, (8, 128), 1) // 32
    quarter16 = lax.broadcasted_iota(jnp.int32, (16, 128), 1) // 32
    quarter128 = lax.broadcasted_iota(jnp.int32, (128, 128), 1) // 32

    loads[0].wait()
    for h in range(2):
        for a in range(4):
            parts = [gains[:, pl.ds(128 * (2 * (4 * a + b) + h), 128)] for b in range(4)]
            for c, y in enumerate(swap_blocks(parts, quarter8)):
                start_send[4 * h + c, :, pl.ds(128 * a, 128)] = y

    pl.semaphore_wait(barrier, 7 + len(NEAR))
    for k in (4, -4):
        signal(entry_sem, at_column(k)[1])

    starts = []
    for k in PLANE:
        t, dev = at_plane(k)
        c = remote(start_send.at[t], start_recv.at[yx], plane_send_sem.at[0, k], plane_recv_sem.at[0, k], dev)
        c.start()
        starts.append(c)
    start_recv[yx] = start_send[yx]

    loads[1].wait()
    row = lax.broadcasted_iota(jnp.int32, (1024, 128), 0)
    chan = ((z + 12 + (row // 512) * 8 + (row // 16) % 8) % 16) * 64 + ((row // 128) % 4) * 16 + row % 16
    for j in range(8):
        onehot[:, pl.ds(128 * j, 128)] = jnp.where(chan == order[pl.ds(j, 1), :], 1.0, 0.0).astype(BF16)
    loads[2].wait()

    def build_matrix(first, last):
        @pl.loop(first, last)
        def _(q):
            rows = pl.ds(pl.multiple_of(q * 256, 256), 256)
            for b in range(4):
                spread[:, pl.ds(256 * b, 256)] = jnp.dot(
                    onehot[rows, pl.ds(256 * b, 256)], blocks[b], preferred_element_type=F32
                ).astype(BF16)
            matrix[rows, :] = lax.dot_general(
                spread[...], onehot[...], NT, preferred_element_type=F32
            ).astype(BF16)

    build_matrix(0, 2)

    for c in starts:
        c.wait()
    pl.semaphore_wait(entry_sem, 2)

    def send_column(copies, ks, it, which, send, at_send, recv, at_recv):
        for k in ks:
            t, dev = at_column(k)
            c = remote(
                send.at[at_send(k)], recv.at[it, at_recv(k)],
                col_send_sem.at[it, which, k], col_recv_sem.at[it, which, k], dev,
            )
            c.start()
            copies[k] = c

    def send_bounds():
        loads[3].wait()
        loads[4].wait()
        i0 = lax.broadcasted_iota(jnp.int32, (8, 128), 0)
        left = lax.broadcasted_iota(jnp.int32, (8, 128), 1) < 64
        tile = jnp.zeros((8, 128), F32)
        for r in range(8):
            tile = jnp.where(i0 == r, jnp.where(left, lower[r], upper[r]), tile)
        bound_send[...] = tile
        copies = []
        for k in PLANE:
            _, dev = at_plane(k)
            c = remote(bound_send, bound_recv.at[yx], plane_send_sem.at[1, k], plane_recv_sem.at[1, k], dev)
            c.start()
            copies.append(c)
        bound_recv[yx] = tile
        return copies

    def prepare_rest():
        loads[7].wait()
        loads[8].wait()
        for src, dst in ((response, resp_tile), (student, stud_tile)):
            x = src[...].astype(F32)
            tall[...] = jnp.transpose(jnp.concatenate([x, x, x, x], axis=0))
            for s in range(16):
                first = ((z + 12 + s) % 16) * 64
                acc = tall[pl.ds(pl.multiple_of(first, 64), 16), :]
                for g in range(1, 4):
                    acc = jnp.where(quarter16 == g, tall[pl.ds(pl.multiple_of(first + 16 * g, 16), 16), :], acc)
                dst[pl.ds(16 * s, 16), :] = acc

    def by_slot(x):
        v = [x[:, 128 * n : 128 * n + 128] for n in range(4)]
        left = lax.broadcasted_iota(jnp.int32, v[0].shape, 1) < 64
        return jnp.concatenate(
            [jnp.where(left, v[a], v[b]) for a, b in ((2, 1), (1, 2), (3, 0), (0, 3))], axis=1
        )

    def prepare_rows():
        loads[5].wait()
        loads[6].wait()
        quarter1 = lax.broadcasted_iota(jnp.int32, (1, 128), 1) // 32
        for src, dst in ((lengths, len_abs), (amplitude, amp_abs)):
            for h in range(2):
                for a in range(4):
                    parts = [src[pl.ds(h + 2 * b + 8 * a, 1), :] for b in range(4)]
                    for c, y in enumerate(swap_blocks(parts, quarter1)):
                        dst[pl.ds(4 * h + c, 1), pl.ds(128 * a, 128)] = y
        turn = ((24 - z) % 16) * 32
        len_all = len_abs[...]
        amp_all = amp_abs[...] * jnp.sqrt(len_all)
        i1 = lax.broadcasted_iota(jnp.int32, (8, 512), 1)
        sq = by_slot(pltpu.roll(len_all * len_all, turn, 1))
        am = by_slot(pltpu.roll(amp_all, turn, 1))
        ps = by_slot((((i1 // 32 + z + 8) % 16) * 256 + i1 % 32).astype(F32))
        for b in range(4):
            part = slice(128 * b, 128 * b + 128)
            sq_t, am_t, ps_t = jnp.transpose(sq[:, part]), jnp.transpose(am[:, part]), jnp.transpose(ps[:, part])
            pos_col[b] = jnp.broadcast_to(ps_t[:, 0:1], (128, 128))
            for t in range(8):
                len_col[t, b] = jnp.broadcast_to(sq_t[:, t : t + 1], (128, 128))
                amp_col[t, b] = jnp.broadcast_to(am_t[:, t : t + 1], (128, 128))
        own_len = len_abs[pl.ds(yx, 1), :]
        own_amp = amp_abs[pl.ds(yx, 1), :]
        own_row[pl.ds(0, 1), :] = own_len * own_len
        own_row[pl.ds(1, 1), :] = own_amp * jnp.sqrt(2.0 * own_len)
        own_row[pl.ds(2, 1), :] = ((i1 // 32) * 256 + i1 % 32 + yx * 32)[0:1].astype(F32)

    def prepare_covar(first, last):
        @pl.loop(first, last)
        def _(t):
            shift = (t * 32).astype(F32)
            for b in range(4):
                rows = pl.ds(pl.multiple_of(512 * t + 128 * b, 128), 128)
                for a in range(4):
                    part = pl.ds(128 * a, 128)
                    inv = lax.rsqrt(len_col[t, b] + own_row[pl.ds(0, 1), part])
                    q = (pos_col[b] - (own_row[pl.ds(2, 1), part] - shift)) * inv
                    vals = (amp_col[t, b] * own_row[pl.ds(1, 1), part]) * (inv * jnp.exp(-(q * q)))
                    covar[rows, part] = vals.astype(BF16)

    def plane_of(k):
        return (z + k) % 16

    def order_of(k):
        return (k + 4) % 16

    def order_from(k):
        return (4 - k) % 16

    def slot_of_piece(k):
        return FROM.index((8 - k) % 16 - 8)

    for it in range(ITERS):
        now = start_recv[...].reshape(64, 512) if it == 0 else state[...]
        for a in range(4):
            parts = [now[16 * g : 16 * g + 16, 128 * a : 128 * a + 128] for g in range(4)]
            for b, y in enumerate(swap_blocks(parts, quarter16)):
                pack_send[4 * a + b] = y.astype(BF16)
        copies = {}
        send_column(copies, FAR + CLOSE, it, 0, pack_send, plane_of, pack_recv, order_from)
        pack_recv[it, 4] = pack_send[z]
        if it == 0:
            bounds = send_bounds()
            build_matrix(2, 4)
            prepare_rest()
            prepare_rows()
            prepare_covar(0, 1)

        def take(half):
            got = pack_recv[it, pl.ds(8 * half, 8)].astype(F32).reshape(128, 128)
            for g in range(4):
                x = jnp.where(quarter128 == g, got, 0.0)
                x = x + pltpu.roll(x, 32, 1)
                x = x + pltpu.roll(x, 64, 1)
                moved[pl.ds(512 * half + 128 * g, 128), :] = x.astype(BF16)

        for k, c in copies.items():
            if order_from(k) < 8:
                c.wait_recv()
        take(0)
        partial[...] = jnp.dot(matrix[:, pl.ds(0, 512)], moved[pl.ds(0, 512), :], preferred_element_type=F32)
        for k, c in copies.items():
            if order_from(k) >= 8:
                c.wait_recv()
        take(1)
        for c in copies.values():
            c.wait_send()
        copies = {}
        for half, ks in ((1, FAR), (0, CLOSE)):
            rows = pl.ds(512 * half, 512)
            full = partial[rows, :] + jnp.dot(
                matrix[rows, pl.ds(512, 512)], moved[pl.ds(512, 512), :], preferred_element_type=F32
            )
            prod = full[0:128]
            for g in range(1, 4):
                prod = jnp.where(quarter128 == g, full[128 * g : 128 * g + 128], prod)
            own = pl.ds(128 * half, 128)
            misfit = (stud_tile[own, :] * (prod - resp_tile[own, :])).astype(BF16)
            mis_send[pl.ds(8 * half, 8)] = misfit.reshape(8, 16, 128)
            send_column(copies, ks, it, 1, mis_send, order_of, mis_recv, slot_of_piece)
        mis_recv[it, slot_of_piece(0)] = mis_send[4]
        if it == 0:
            prepare_covar(1, 3)

        forwards = []
        for part in range(4):
            for k, c in copies.items():
                if slot_of_piece(k) // 4 == part:
                    c.wait_recv()
            parts = [mis_recv[it, 4 * part + b].astype(F32) for b in range(4)]
            for g, y in enumerate(swap_blocks(parts, quarter16)):
                gathered[it, yx, part, pl.ds(16 * g, 16), :] = y.astype(BF16)
            sent = []
            for k in PLANE:
                t, dev = at_plane(k)
                c = remote(
                    gathered.at[it, yx, part], gathered.at[it, yx, part],
                    ag_send_sem.at[it, part, k], ag_recv_sem.at[it, part, k], dev,
                )
                c.start()
                sent.append(c)
            forwards.append(sent)
            if it == 0 and part == 1:
                prepare_covar(3, 5)
        if it == 0:
            prepare_covar(5, 8)

        smoothed = None
        for parts in ((0, 1), (2,), (3,)):
            for n in range(0, 8, 3 - len(parts)):
                left, right = [], []
                for m in range(n, n + 3 - len(parts)):
                    t = at_plane(PLANE[-m], -1)[0] if m else yx
                    for part in parts:
                        if m:
                            forwards[part][-m].wait_recv()
                        left.append(gathered[it, t, part])
                        right.append(covar[pl.ds(pl.multiple_of(512 * t + 128 * part, 128), 128), :])
                p = jnp.dot(
                    jnp.concatenate(left, axis=1), jnp.concatenate(right, axis=0), preferred_element_type=F32
                )
                smoothed = p if smoothed is None else smoothed + p
        if it == 0:
            for c in bounds:
                c.wait()
        edge = bound_recv[...].reshape(64, 128)
        lo = jnp.broadcast_to(edge[:, 0:1], (64, 512))
        hi = jnp.broadcast_to(edge[:, 64:65], (64, 512))
        now = start_recv[...].reshape(64, 512) if it == 0 else state[...]
        nxt = jnp.minimum(jnp.maximum(now - 0.02 * smoothed, lo), hi)
        if it < ITERS - 1:
            state[...] = nxt
        else:
            final_send[...] = nxt.reshape(8, 8, 512)
        for c in copies.values():
            c.wait_send()
        for sent in forwards:
            for c in sent:
                c.wait_send()

    copies = []
    for k in PLANE:
        t, dev = at_plane(k)
        c = remote(final_send.at[t], final_recv.at[yx], plane_send_sem.at[2, k], plane_recv_sem.at[2, k], dev)
        c.start()
        copies.append(c)
    final_recv[yx] = final_send[yx]
    for c in copies:
        c.wait()
    for h in range(2):
        for a in range(4):
            parts = [final_recv[4 * h + c, :, pl.ds(128 * a, 128)] for c in range(4)]
            for b, y in enumerate(swap_blocks(parts, quarter8)):
                out[:, pl.ds(128 * (2 * (4 * a + b) + h), 128)] = y


def per_device(gains, response, student, blocks, order, lower, upper, lengths, amplitude):
    hbm = pl.BlockSpec(memory_space=pltpu.HBM)
    return pl.pallas_call(
        kernel,
        out_shape=jax.ShapeDtypeStruct((8, 4096), F32),
        in_specs=[hbm] * 9,
        out_specs=pl.BlockSpec(memory_space=pltpu.VMEM),
        scratch_shapes=[
            pltpu.VMEM((8, 4096), F32),
            pltpu.SMEM((8,), F32),
            pltpu.SMEM((8,), F32),
            pltpu.VMEM((32, 1024), BF16),
            pltpu.VMEM((32, 1024), BF16),
            pltpu.VMEM((4, 256, 256), BF16),
            pltpu.VMEM((8, 128), jnp.int32),
            pltpu.VMEM((32, 128), F32),
            pltpu.VMEM((32, 128), F32),
            pltpu.VMEM((8, 8, 512), F32),
            pltpu.VMEM((8, 8, 512), F32),
            pltpu.VMEM((8, 128), F32),
            pltpu.VMEM((8, 8, 128), F32),
            pltpu.VMEM((64, 512), F32),
            pltpu.VMEM((16, 16, 128), BF16),
            pltpu.VMEM((ITERS, 16, 16, 128), BF16),
            pltpu.VMEM((16, 16, 128), BF16),
            pltpu.VMEM((ITERS, 16, 16, 128), BF16),
            pltpu.VMEM((ITERS, 8, 4, 64, 128), BF16),
            pltpu.VMEM((8, 8, 512), F32),
            pltpu.VMEM((8, 8, 512), F32),
            pltpu.VMEM((1024, 1024), BF16),
            pltpu.VMEM((1024, 1024), BF16),
            pltpu.VMEM((1024, 128), BF16),
            pltpu.VMEM((1024, 128), F32),
            pltpu.VMEM((1024, 128), F32),
            pltpu.VMEM((256, 128), F32),
            pltpu.VMEM((256, 128), F32),
            pltpu.VMEM((256, 1024), BF16),
            pltpu.VMEM((4096, 512), BF16),
            pltpu.VMEM((8, 512), F32),
            pltpu.VMEM((8, 512), F32),
            pltpu.VMEM((8, 512), F32),
            pltpu.VMEM((8, 4, 128, 128), F32),
            pltpu.VMEM((8, 4, 128, 128), F32),
            pltpu.VMEM((4, 128, 128), F32),
            pltpu.SemaphoreType.DMA((9,)),
            pltpu.SemaphoreType.REGULAR,
            pltpu.SemaphoreType.DMA((3, 8)),
            pltpu.SemaphoreType.DMA((3, 8)),
            pltpu.SemaphoreType.DMA((ITERS, 4, 8)),
            pltpu.SemaphoreType.DMA((ITERS, 4, 8)),
            pltpu.SemaphoreType.DMA((ITERS, 2, 16)),
            pltpu.SemaphoreType.DMA((ITERS, 2, 16)),
        ],
        compiler_params=pltpu.CompilerParams(collective_id=0, has_side_effects=True, vmem_limit_bytes=24 << 20),
        name="track",
    )(*[
        pltpu.with_memory_space_constraint(v, pltpu.HBM)
        for v in (
            gains, lower, upper, response, student, blocks,
            order.reshape(8, 128), lengths.reshape(32, 128), amplitude.reshape(32, 128),
        )
    ])


def solution(mesh):
    placed = (
        P(("half", "wide"), None),
        P("wide", "half"),
        P("wide", "half"),
        P("half", None, None),
        P("half"),
        P(("half", "wide")),
        P(("half", "wide")),
        P(),
        P(),
    )
    return jax.shard_map(
        per_device, mesh=mesh, in_specs=placed, out_specs=P(("half", "wide"), None), check_vma=False
    )
```

```python
import functools

import jax
import jax.numpy as jnp
from jax import lax
from jax.experimental import pallas as pl
from jax.experimental.pallas import tpu as pltpu
from jax.sharding import PartitionSpec as P

ITERS = 2
F32 = jnp.float32
BF16 = jnp.bfloat16
NEAR = (-4, 4, -3, 3, -2, 2, -1, 1)
FAR = (8, 7, 9, 6, 10, 5, 11, 4)
CLOSE = (12, 3, 13, 2, 14, 1, 15)
PLANE = (5, 4, 3, 7, 2, 6, 1)
FROM = (0, 1, -2, -1, -4, -3, 2, 3, 4, 5, -6, -5, -8, -7, 6, 7)
NT = (((1,), (1,)), ((), ()))


def swap_blocks(parts, quarter):
    out = []
    for b in range(4):
        acc = None
        for g in range(4):
            moved = parts[g] if g == b else pltpu.roll(parts[g], (32 * (g - b)) % 128, 1)
            acc = moved if acc is None else jnp.where(quarter == g, moved, acc)
        out.append(acc)
    return out


def kernel(
    gains_hbm, lower_hbm, upper_hbm, response_hbm, student_hbm, blocks_hbm, order_hbm, lengths_hbm, amplitude_hbm,
    out,
    gains, lower, upper, response, student, blocks, order, lengths, amplitude,
    start_send, start_recv, bound_send, bound_recv, state,
    pack_send, pack_recv, mis_send, mis_recv, gathered, final_send, final_recv,
    onehot, matrix, moved, partial, tall, resp_tile, stud_tile, spread, covar, len_abs, amp_abs, own_row, len_col, amp_col, pos_col,
    load_sem, entry_sem, plane_send_sem, plane_recv_sem, ag_send_sem, ag_recv_sem, col_send_sem, col_recv_sem,
):
    wide = lax.axis_index("wide")
    z = wide // 8
    yx = wide % 8

    def at_plane(k, sign=1):
        t = ((yx // 2 + sign * (k // 2) + 4) % 4) * 2 + (yx % 2 + k) % 2
        return t, {"wide": z * 8 + t}

    def at_column(k):
        t = (z + k + 16) % 16
        return t, {"wide": t * 8 + yx}

    def signal(sem, dev):
        pl.semaphore_signal(sem, inc=1, device_id=dev, device_id_type=pl.DeviceIdType.MESH)

    barrier = pltpu.get_barrier_semaphore()
    for k in NEAR:
        signal(barrier, at_column(k)[1])
    for k in PLANE:
        signal(barrier, at_plane(k)[1])

    loads = []
    for n, (src, dst) in enumerate((
        (gains_hbm, gains), (order_hbm, order), (blocks_hbm, blocks), (lower_hbm, lower), (upper_hbm, upper),
        (lengths_hbm, lengths), (amplitude_hbm, amplitude), (response_hbm, response), (student_hbm, student),
    )):
        c = pltpu.make_async_copy(src, dst, load_sem.at[n])
        c.start()
        loads.append(c)

    def remote(src, dst, ssem, rsem, dev):
        return pltpu.make_async_remote_copy(
            src_ref=src, dst_ref=dst, send_sem=ssem, recv_sem=rsem,
            device_id=dev, device_id_type=pl.DeviceIdType.MESH,
        )

    quarter8 = lax.broadcasted_iota(jnp.int32, (8, 128), 1) // 32
    quarter16 = lax.broadcasted_iota(jnp.int32, (16, 128), 1) // 32
    quarter128 = lax.broadcasted_iota(jnp.int32, (128, 128), 1) // 32

    loads[0].wait()
    for h in range(2):
        for a in range(4):
            parts = [gains[:, pl.ds(128 * (2 * (4 * a + b) + h), 128)] for b in range(4)]
            for c, y in enumerate(swap_blocks(parts, quarter8)):
                start_send[4 * h + c, :, pl.ds(128 * a, 128)] = y

    pl.semaphore_wait(barrier, 7 + len(NEAR))
    for k in (4, -4):
        signal(entry_sem, at_column(k)[1])

    starts = []
    for k in PLANE:
        t, dev = at_plane(k)
        c = remote(start_send.at[t], start_recv.at[yx], plane_send_sem.at[0, k], plane_recv_sem.at[0, k], dev)
        c.start()
        starts.append(c)
    start_recv[yx] = start_send[yx]

    loads[1].wait()
    row = lax.broadcasted_iota(jnp.int32, (1024, 128), 0)
    chan = ((z + 12 + (row // 512) * 8 + (row // 16) % 8) % 16) * 64 + ((row // 128) % 4) * 16 + row % 16
    for j in range(8):
        onehot[:, pl.ds(128 * j, 128)] = jnp.where(chan == order[pl.ds(j, 1), :], 1.0, 0.0).astype(BF16)
    loads[2].wait()

    def build_matrix(first, last):
        @pl.loop(first, last)
        def _(q):
            rows = pl.ds(pl.multiple_of(q * 256, 256), 256)
            for b in range(4):
                spread[:, pl.ds(256 * b, 256)] = jnp.dot(
                    onehot[rows, pl.ds(256 * b, 256)], blocks[b], preferred_element_type=F32
                ).astype(BF16)
            matrix[rows, :] = lax.dot_general(
                spread[...], onehot[...], NT, preferred_element_type=F32
            ).astype(BF16)

    build_matrix(0, 2)

    for c in starts:
        c.wait()
    pl.semaphore_wait(entry_sem, 2)

    def send_column(copies, ks, it, which, send, at_send, recv, at_recv):
        for k in ks:
            t, dev = at_column(k)
            c = remote(
                send.at[at_send(k)], recv.at[it, at_recv(k)],
                col_send_sem.at[it, which, k], col_recv_sem.at[it, which, k], dev,
            )
            c.start()
            copies[k] = c

    def send_bounds():
        loads[3].wait()
        loads[4].wait()
        i0 = lax.broadcasted_iota(jnp.int32, (8, 128), 0)
        left = lax.broadcasted_iota(jnp.int32, (8, 128), 1) < 64
        tile = jnp.zeros((8, 128), F32)
        for r in range(8):
            tile = jnp.where(i0 == r, jnp.where(left, lower[r], upper[r]), tile)
        bound_send[...] = tile
        copies = []
        for k in PLANE:
            _, dev = at_plane(k)
            c = remote(bound_send, bound_recv.at[yx], plane_send_sem.at[1, k], plane_recv_sem.at[1, k], dev)
            c.start()
            copies.append(c)
        bound_recv[yx] = tile
        return copies

    def prepare_rest():
        loads[7].wait()
        loads[8].wait()
        for src, dst in ((response, resp_tile), (student, stud_tile)):
            x = src[...].astype(F32)
            tall[...] = jnp.transpose(jnp.concatenate([x, x, x, x], axis=0))
            for s in range(16):
                first = ((z + 12 + s) % 16) * 64
                acc = tall[pl.ds(pl.multiple_of(first, 64), 16), :]
                for g in range(1, 4):
                    acc = jnp.where(quarter16 == g, tall[pl.ds(pl.multiple_of(first + 16 * g, 16), 16), :], acc)
                dst[pl.ds(16 * s, 16), :] = acc

    def by_slot(x):
        v = [x[:, 128 * n : 128 * n + 128] for n in range(4)]
        left = lax.broadcasted_iota(jnp.int32, v[0].shape, 1) < 64
        return jnp.concatenate(
            [jnp.where(left, v[a], v[b]) for a, b in ((2, 1), (1, 2), (3, 0), (0, 3))], axis=1
        )

    def prepare_rows():
        loads[5].wait()
        loads[6].wait()
        quarter1 = lax.broadcasted_iota(jnp.int32, (1, 128), 1) // 32
        for src, dst in ((lengths, len_abs), (amplitude, amp_abs)):
            for h in range(2):
                for a in range(4):
                    parts = [src[pl.ds(h + 2 * b + 8 * a, 1), :] for b in range(4)]
                    for c, y in enumerate(swap_blocks(parts, quarter1)):
                        dst[pl.ds(4 * h + c, 1), pl.ds(128 * a, 128)] = y
        turn = ((24 - z) % 16) * 32
        len_all = len_abs[...]
        amp_all = amp_abs[...] * jnp.sqrt(len_all)
        i1 = lax.broadcasted_iota(jnp.int32, (8, 512), 1)
        sq = by_slot(pltpu.roll(len_all * len_all, turn, 1))
        am = by_slot(pltpu.roll(amp_all, turn, 1))
        ps = by_slot((((i1 // 32 + z + 8) % 16) * 256 + i1 % 32).astype(F32))
        for b in range(4):
            part = slice(128 * b, 128 * b + 128)
            sq_t, am_t, ps_t = jnp.transpose(sq[:, part]), jnp.transpose(am[:, part]), jnp.transpose(ps[:, part])
            pos_col[b] = jnp.broadcast_to(ps_t[:, 0:1], (128, 128))
            for t in range(8):
                len_col[t, b] = jnp.broadcast_to(sq_t[:, t : t + 1], (128, 128))
                amp_col[t, b] = jnp.broadcast_to(am_t[:, t : t + 1], (128, 128))
        own_len = len_abs[pl.ds(yx, 1), :]
        own_amp = amp_abs[pl.ds(yx, 1), :]
        own_row[pl.ds(0, 1), :] = own_len * own_len
        own_row[pl.ds(1, 1), :] = own_amp * jnp.sqrt(2.0 * own_len)
        own_row[pl.ds(2, 1), :] = ((i1 // 32) * 256 + i1 % 32 + yx * 32)[0:1].astype(F32)

    def prepare_covar(first, last):
        @pl.loop(first, last)
        def _(t):
            shift = (t * 32).astype(F32)
            for b in range(4):
                rows = pl.ds(pl.multiple_of(512 * t + 128 * b, 128), 128)
                for a in range(4):
                    part = pl.ds(128 * a, 128)
                    inv = lax.rsqrt(len_col[t, b] + own_row[pl.ds(0, 1), part])
                    q = (pos_col[b] - (own_row[pl.ds(2, 1), part] - shift)) * inv
                    vals = (amp_col[t, b] * own_row[pl.ds(1, 1), part]) * (inv * jnp.exp(-(q * q)))
                    covar[rows, part] = vals.astype(BF16)

    def plane_of(k):
        return (z + k) % 16

    def order_of(k):
        return (k + 4) % 16

    def order_from(k):
        return (4 - k) % 16

    def slot_of_piece(k):
        return FROM.index((8 - k) % 16 - 8)

    pending = []
    for it in range(ITERS):
        now = start_recv[...].reshape(64, 512) if it == 0 else state[...]
        for a in range(4):
            parts = [now[16 * g : 16 * g + 16, 128 * a : 128 * a + 128] for g in range(4)]
            for b, y in enumerate(swap_blocks(parts, quarter16)):
                pack_send[4 * a + b] = y.astype(BF16)
        copies = {}
        send_column(copies, FAR + CLOSE, it, 0, pack_send, plane_of, pack_recv, order_from)
        pack_recv[it, 4] = pack_send[z]
        for c in pending:
            c.wait_send()
        if it == 0:
            bounds = send_bounds()
            build_matrix(2, 4)
            prepare_rest()
            prepare_rows()
            prepare_covar(0, 1)

        def take(half):
            got = pack_recv[it, pl.ds(8 * half, 8)].astype(F32).reshape(128, 128)
            for g in range(4):
                x = jnp.where(quarter128 == g, got, 0.0)
                x = x + pltpu.roll(x, 32, 1)
                x = x + pltpu.roll(x, 64, 1)
                moved[pl.ds(512 * half + 128 * g, 128), :] = x.astype(BF16)

        for k, c in copies.items():
            if order_from(k) < 8:
                c.wait_recv()
        take(0)
        partial[...] = jnp.dot(matrix[:, pl.ds(0, 512)], moved[pl.ds(0, 512), :], preferred_element_type=F32)
        for k, c in copies.items():
            if order_from(k) >= 8:
                c.wait_recv()
        take(1)
        for c in copies.values():
            c.wait_send()
        copies = {}
        for half, ks in ((1, FAR), (0, CLOSE)):
            rows = pl.ds(512 * half, 512)
            full = partial[rows, :] + jnp.dot(
                matrix[rows, pl.ds(512, 512)], moved[pl.ds(512, 512), :], preferred_element_type=F32
            )
            prod = full[0:128]
            for g in range(1, 4):
                prod = jnp.where(quarter128 == g, full[128 * g : 128 * g + 128], prod)
            own = pl.ds(128 * half, 128)
            misfit = (stud_tile[own, :] * (prod - resp_tile[own, :])).astype(BF16)
            mis_send[pl.ds(8 * half, 8)] = misfit.reshape(8, 16, 128)
            send_column(copies, ks, it, 1, mis_send, order_of, mis_recv, slot_of_piece)
        mis_recv[it, slot_of_piece(0)] = mis_send[4]
        if it == 0:
            prepare_covar(1, 3)

        forwards = []
        for part in range(4):
            for k, c in copies.items():
                if slot_of_piece(k) // 4 == part:
                    c.wait_recv()
            parts = [mis_recv[it, 4 * part + b].astype(F32) for b in range(4)]
            for g, y in enumerate(swap_blocks(parts, quarter16)):
                gathered[it, yx, part, pl.ds(16 * g, 16), :] = y.astype(BF16)
            sent = []
            for k in PLANE:
                t, dev = at_plane(k)
                c = remote(
                    gathered.at[it, yx, part], gathered.at[it, yx, part],
                    ag_send_sem.at[it, part, k], ag_recv_sem.at[it, part, k], dev,
                )
                c.start()
                sent.append(c)
            forwards.append(sent)
            if it == 0 and part == 1:
                prepare_covar(3, 5)
        if it == 0:
            prepare_covar(5, 8)

        smoothed = None
        for parts in ((0, 1), (2,), (3,)):
            for n in range(0, 8, 3 - len(parts)):
                left, right = [], []
                for m in range(n, n + 3 - len(parts)):
                    t = at_plane(PLANE[-m], -1)[0] if m else yx
                    for part in parts:
                        if m:
                            forwards[part][-m].wait_recv()
                        left.append(gathered[it, t, part])
                        right.append(covar[pl.ds(pl.multiple_of(512 * t + 128 * part, 128), 128), :])
                p = jnp.dot(
                    jnp.concatenate(left, axis=1), jnp.concatenate(right, axis=0), preferred_element_type=F32
                )
                smoothed = p if smoothed is None else smoothed + p
        if it == 0:
            for c in bounds:
                c.wait()
        edge = bound_recv[...].reshape(64, 128)
        lo = jnp.broadcast_to(edge[:, 0:1], (64, 512))
        hi = jnp.broadcast_to(edge[:, 64:65], (64, 512))
        now = start_recv[...].reshape(64, 512) if it == 0 else state[...]
        nxt = jnp.minimum(jnp.maximum(now - 0.02 * smoothed, lo), hi)
        if it < ITERS - 1:
            state[...] = nxt
        else:
            final_send[...] = nxt.reshape(8, 8, 512)
        pending = list(copies.values()) + [c for sent in forwards for c in sent]

    copies = []
    for k in PLANE:
        t, dev = at_plane(k)
        c = remote(final_send.at[t], final_recv.at[yx], plane_send_sem.at[2, k], plane_recv_sem.at[2, k], dev)
        c.start()
        copies.append(c)
    final_recv[yx] = final_send[yx]
    for c in pending:
        c.wait_send()
    for c in copies:
        c.wait()
    for h in range(2):
        for a in range(4):
            parts = [final_recv[4 * h + c, :, pl.ds(128 * a, 128)] for c in range(4)]
            for b, y in enumerate(swap_blocks(parts, quarter8)):
                out[:, pl.ds(128 * (2 * (4 * a + b) + h), 128)] = y


def per_device(gains, response, student, blocks, order, lower, upper, lengths, amplitude):
    hbm = pl.BlockSpec(memory_space=pltpu.HBM)
    return pl.pallas_call(
        kernel,
        out_shape=jax.ShapeDtypeStruct((8, 4096), F32),
        in_specs=[hbm] * 9,
        out_specs=pl.BlockSpec(memory_space=pltpu.VMEM),
        scratch_shapes=[
            pltpu.VMEM((8, 4096), F32),
            pltpu.SMEM((8,), F32),
            pltpu.SMEM((8,), F32),
            pltpu.VMEM((32, 1024), BF16),
            pltpu.VMEM((32, 1024), BF16),
            pltpu.VMEM((4, 256, 256), BF16),
            pltpu.VMEM((8, 128), jnp.int32),
            pltpu.VMEM((32, 128), F32),
            pltpu.VMEM((32, 128), F32),
            pltpu.VMEM((8, 8, 512), F32),
            pltpu.VMEM((8, 8, 512), F32),
            pltpu.VMEM((8, 128), F32),
            pltpu.VMEM((8, 8, 128), F32),
            pltpu.VMEM((64, 512), F32),
            pltpu.VMEM((16, 16, 128), BF16),
            pltpu.VMEM((ITERS, 16, 16, 128), BF16),
            pltpu.VMEM((16, 16, 128), BF16),
            pltpu.VMEM((ITERS, 16, 16, 128), BF16),
            pltpu.VMEM((ITERS, 8, 4, 64, 128), BF16),
            pltpu.VMEM((8, 8, 512), F32),
            pltpu.VMEM((8, 8, 512), F32),
            pltpu.VMEM((1024, 1024), BF16),
            pltpu.VMEM((1024, 1024), BF16),
            pltpu.VMEM((1024, 128), BF16),
            pltpu.VMEM((1024, 128), F32),
            pltpu.VMEM((1024, 128), F32),
            pltpu.VMEM((256, 128), F32),
            pltpu.VMEM((256, 128), F32),
            pltpu.VMEM((256, 1024), BF16),
            pltpu.VMEM((4096, 512), BF16),
            pltpu.VMEM((8, 512), F32),
            pltpu.VMEM((8, 512), F32),
            pltpu.VMEM((8, 512), F32),
            pltpu.VMEM((8, 4, 128, 128), F32),
            pltpu.VMEM((8, 4, 128, 128), F32),
            pltpu.VMEM((4, 128, 128), F32),
            pltpu.SemaphoreType.DMA((9,)),
            pltpu.SemaphoreType.REGULAR,
            pltpu.SemaphoreType.DMA((3, 8)),
            pltpu.SemaphoreType.DMA((3, 8)),
            pltpu.SemaphoreType.DMA((ITERS, 4, 8)),
            pltpu.SemaphoreType.DMA((ITERS, 4, 8)),
            pltpu.SemaphoreType.DMA((ITERS, 2, 16)),
            pltpu.SemaphoreType.DMA((ITERS, 2, 16)),
        ],
        compiler_params=pltpu.CompilerParams(collective_id=0, has_side_effects=True, vmem_limit_bytes=24 << 20),
        name="track",
    )(*[
        pltpu.with_memory_space_constraint(v, pltpu.HBM)
        for v in (
            gains, lower, upper, response, student, blocks,
            order.reshape(8, 128), lengths.reshape(32, 128), amplitude.reshape(32, 128),
        )
    ])


def solution(mesh):
    placed = (
        P(("half", "wide"), None),
        P("wide", "half"),
        P("wide", "half"),
        P("half", None, None),
        P("half"),
        P(("half", "wide")),
        P(("half", "wide")),
        P(),
        P(),
    )
    return jax.shard_map(
        per_device, mesh=mesh, in_specs=placed, out_specs=P(("half", "wide"), None), check_vma=False
    )
```
